128 devices in a mesh: neuron: 16 (over z, y), trial: 8 (over x, core).
Axes of the slice: x: 4, y: 4, z: 4, core: 2. Of those that a mesh axis runs over, the one named last changes fastest.
Arguments:
- drive: bfloat16 [8, 128, 131072], P(None, 'trial', 'neuron'), may hold values from -6 to 6
- learning: bfloat16 [8, 128, 131072], P(None, 'trial', 'neuron'), may hold values from -6 to 6
- membrane_init: float32 [128, 131072], P('trial', 'neuron'), may hold values from -3 to 3
- adapt_init: float32 [128, 131072], P('trial', 'neuron'), may hold values from 0 to 1
- trace_init: float32 [128, 131072], P('trial', 'neuron'), may hold values from 0 to 3
- membrane_decay: float32 [131072], P('neuron'), may hold values from 0.6 to 0.95
- adapt_decay: float32 [131072], P('neuron'), may hold values from 0.8 to 0.99
- adapt_gain: float32 [131072], P('neuron'), may hold values from 0.2 to 1
- threshold: float32 [131072], P('neuron'), may hold values from 0.5 to 1.5
- left_factor: bfloat16 [131072, 512], P('neuron'), may hold values from -6 to 6
- right_factor: bfloat16 [131072, 512], P('neuron'), may hold values from -16 to 16
Outputs:
- left_new: bfloat16 [131072, 512], P(('neuron', 'trial'))
- right_new: bfloat16 [131072, 512], P(('neuron', 'trial'))
The draws below stay inside these ranges and needn't reach their ends.
All inputs are finite; a program needn't handle non-finite values.
Results may differ from the reference program's by a relative error of at most 0.0085.
Values may be sent and summed in bfloat16 or wider, within the bound.
No kernel may reach another device: no remote copies, remote signals or barrier semaphores. Data moves between devices by JAX's collectives and lax.ppermute only.
A program may use at most 128 MiB of HBM per device.

```python
import math
import jax
import jax.numpy as jnp
from jax import lax

NEURONS = 131072
RANK = 512
STEPS = 8
TRIALS = 128


def draw_right_factor(key, part):
    key_rows = jax.random.fold_in(key, 11)
    key_vals = jax.random.fold_in(key, 23)
    position = jnp.arange(NEURONS, dtype=jnp.float32) / NEURONS
    rising = jnp.exp(position * jnp.log(6.0)) / 3.0
    rough = jnp.exp(jax.random.uniform(key_rows, (NEURONS,), jnp.float32, 0.0, jnp.log(2.0)))
    scale = (rising * rough)[:, None]
    values = jax.random.truncated_normal(key_vals, -4.0, 4.0, (NEURONS, RANK), jnp.float32)
    return (values * scale).astype(jnp.bfloat16)


def levels(key, shape, shards, low, high):
    loudness, own = 1.0, jax.random.fold_in(key, 6)
    for axis_at, shards_of in shards:
        steps = jnp.exp(jax.random.uniform(jax.random.fold_in(own, axis_at), (shards_of,), jnp.float32, low / len(shards), high / len(shards)))
        loudness = loudness * jnp.repeat(steps, shape[axis_at] // shards_of).reshape([-1 if axis == axis_at else 1 for axis in range(len(shape))])
    return loudness


def centred(own_key, shape, scale, limit, pieces=(), kind=jnp.bfloat16):
    factor_of = levels(own_key, shape, pieces, -0.22, 0.18) if pieces else 1.0
    entries = jax.random.normal(own_key, shape, jnp.float32) * scale * factor_of
    return jnp.minimum(jnp.maximum(entries, -limit), limit).astype(kind)


def setup_inputs(seed: int = 0) -> dict:
    key_list = jax.random.split(jax.random.key(seed), 12)
    return {
        "drive": centred(key_list[0], (STEPS, TRIALS, NEURONS), 1.0, 6.0, ((1, 8), (2, 16))),
        "learning": centred(key_list[1], (STEPS, TRIALS, NEURONS), 1.0, 6.0, ((1, 8), (2, 16))),
        "membrane_init": centred(key_list[2], (TRIALS, NEURONS), 0.5, 3.0, ((0, 8), (1, 16)), jnp.float32),
        "adapt_init": jnp.clip(1.0 * jax.random.uniform(key_list[3], (TRIALS, NEURONS), jnp.float32) ** levels(key_list[3], (TRIALS, NEURONS), ((0, 8), (1, 16)), -0.2, 0.2), 0.0, 1.0),
        "trace_init": jnp.clip(3.0 * jax.random.uniform(key_list[4], (TRIALS, NEURONS), jnp.float32) ** levels(key_list[4], (TRIALS, NEURONS), ((0, 8), (1, 16)), -0.2, 0.2), 0.0, 3.0),
        "membrane_decay": jnp.clip(0.6 + 0.34999996 * jax.random.uniform(key_list[5], (NEURONS,), jnp.float32) ** levels(key_list[5], (NEURONS,), ((0, 16),), -0.2, 0.2), 0.6, 0.95),
        "adapt_decay": jnp.clip(0.8 + 0.19 * jax.random.uniform(key_list[6], (NEURONS,), jnp.float32) ** levels(key_list[6], (NEURONS,), ((0, 16),), -0.2, 0.2), 0.8, 0.99),
        "adapt_gain": jnp.clip(0.2 + 0.8 * jax.random.uniform(key_list[7], (NEURONS,), jnp.float32) ** levels(key_list[7], (NEURONS,), ((0, 16),), -0.2, 0.2), 0.2, 1.0),
        "threshold": jnp.clip(0.5 + 1.0 * jax.random.uniform(key_list[8], (NEURONS,), jnp.float32) ** levels(key_list[8], (NEURONS,), ((0, 16),), -0.2, 0.2), 0.5, 1.5),
        "left_factor": centred(key_list[9], (NEURONS, RANK), 1.0, 6.0, ((0, 16),)),
        "right_factor": draw_right_factor(jax.random.fold_in(key_list[11], 71), 0),
    }


sharpness = 3.0
learn_rate = 0.5

def reference(drive, learning, membrane_init, adapt_init, trace_init, membrane_decay, adapt_decay, adapt_gain, threshold, left_factor, right_factor):
    norm_neurons = 1.0 / math.sqrt(NEURONS)
    norm_rank = 1.0 / math.sqrt(RANK)
    membrane = membrane_init
    adaptation = adapt_init
    filtered = trace_init
    spikes = jax.nn.sigmoid(sharpness * (membrane - threshold - adapt_gain * adaptation))
    signals = []
    presyns = []
    for moment in range(STEPS):
        partial_value = jnp.dot(spikes.astype(jnp.bfloat16).astype(jnp.float32), right_factor.astype(jnp.float32), preferred_element_type=jnp.float32) * norm_neurons
        projected = partial_value.astype(jnp.bfloat16)
        current = lax.dot_general(projected.astype(jnp.float32), left_factor.astype(jnp.float32), (((1,), (1,)), ((), ())), preferred_element_type=jnp.float32) * norm_rank
        membrane = membrane_decay * membrane + drive[moment].astype(jnp.float32) + current - threshold * spikes
        adaptation = adapt_decay * adaptation + spikes
        spikes = jax.nn.sigmoid(sharpness * (membrane - threshold - adapt_gain * adaptation))
        slope_value = sharpness * spikes * (1.0 - spikes)
        filtered = membrane_decay * filtered + spikes
        signals.append((learning[moment].astype(jnp.float32) * slope_value).astype(jnp.bfloat16))
        presyns.append(filtered.astype(jnp.bfloat16))
    signal_all = jnp.stack(signals).reshape(-1, NEURONS)
    presyn_all = jnp.stack(presyns).reshape(-1, NEURONS)
    rank_g = (jnp.dot(presyn_all.astype(jnp.float32), right_factor.astype(jnp.float32), preferred_element_type=jnp.float32) * norm_neurons).astype(jnp.bfloat16)
    rank_k = (jnp.dot(signal_all.astype(jnp.float32), left_factor.astype(jnp.float32), preferred_element_type=jnp.float32) * norm_neurons).astype(jnp.bfloat16)
    lead = (((0,), (0,)), ((), ()))
    grad_left = lax.dot_general(signal_all.astype(jnp.float32), rank_g.astype(jnp.float32), lead, preferred_element_type=jnp.float32) * norm_rank
    grad_right = lax.dot_general(presyn_all.astype(jnp.float32), rank_k.astype(jnp.float32), lead, preferred_element_type=jnp.float32) * norm_rank
    left_step = left_factor.astype(jnp.float32) - learn_rate * grad_left
    right_step = right_factor.astype(jnp.float32) - learn_rate * grad_right
    highest = lax.Precision.HIGHEST
    gram_one = lax.dot_general(right_step, right_step, lead, precision=highest)
    lower_one = jnp.linalg.cholesky(gram_one)
    basis = lax.linalg.triangular_solve(lower_one, right_step, left_side=False, lower=True, transpose_a=True)
    right_new = (basis * math.sqrt(NEURONS)).astype(jnp.bfloat16)
    left_new = (jnp.dot(left_step, lower_one, precision=highest) * norm_neurons).astype(jnp.bfloat16)
    return (left_new, right_new)
```

```python
import math

import jax
import jax.numpy as jnp
from jax import lax
from jax.sharding import PartitionSpec as P

sharpness = 3.0
learn_rate = 0.5


def rank_block(values, factor, weight):
    return jnp.dot(values, factor, preferred_element_type=jnp.float32) * weight


def swap(values, axes):
    return lax.all_to_all(values, axes, split_axis=0, concat_axis=0, tiled=True)


def spread(values, axes):
    copies = math.prod(lax.axis_size(a) for a in ((axes,) if isinstance(axes, str) else axes))
    return swap(jnp.broadcast_to(values[None], (copies,) + values.shape), axes)


def total(partial_value, axes):
    return jnp.sum(spread(partial_value.astype(jnp.bfloat16), axes).astype(jnp.float32), 0)


def shards(
    drive,
    learning,
    membrane_init,
    adapt_init,
    trace_init,
    membrane_decay,
    adapt_decay,
    adapt_gain,
    threshold,
    left_factor,
    right_factor,
):
    local_neurons = left_factor.shape[0]
    rank_width = left_factor.shape[1]
    step_count, local_trials = drive.shape[:2]
    neuron_shards = lax.axis_size("neuron")
    trial_shards = lax.axis_size("trial")
    neuron_count = local_neurons * neuron_shards
    norm_neurons = 1.0 / math.sqrt(neuron_count)
    norm_rank = 1.0 / math.sqrt(rank_width)
    membrane = membrane_init
    adaptation = adapt_init
    filtered = trace_init
    spikes = jax.nn.sigmoid(sharpness * (membrane - threshold - adapt_gain * adaptation))
    signals = []
    presyns = []
    for moment in range(step_count):
        partial_value = rank_block(spikes.astype(jnp.bfloat16), right_factor, norm_neurons)
        projected = total(partial_value, "neuron").astype(jnp.bfloat16)
        current = (
            lax.dot_general(
                projected, left_factor, (((1,), (1,)), ((), ())), preferred_element_type=jnp.float32
            )
            * norm_rank
        )
        membrane = (
            membrane_decay * membrane
            + drive[moment].astype(jnp.float32)
            + current
            - threshold * spikes
        )
        adaptation = adapt_decay * adaptation + spikes
        spikes = jax.nn.sigmoid(sharpness * (membrane - threshold - adapt_gain * adaptation))
        slope_value = sharpness * spikes * (1.0 - spikes)
        filtered = membrane_decay * filtered + spikes
        signals.append((learning[moment].astype(jnp.float32) * slope_value).astype(jnp.bfloat16))
        presyns.append(filtered.astype(jnp.bfloat16))
    rows = step_count * local_trials
    stored = local_neurons // trial_shards
    signal_all = jnp.concatenate(signals)
    presyn_all = jnp.concatenate(presyns)
    g_part = rank_block(presyn_all, right_factor, norm_neurons)
    k_part = rank_block(signal_all, left_factor, norm_neurons)
    both = jnp.concatenate([g_part, k_part]).astype(jnp.bfloat16)
    mine = swap(both.reshape(neuron_shards, -1, rank_width), "neuron")
    mine = jnp.sum(mine.astype(jnp.float32), 0).astype(jnp.bfloat16)
    ranks = spread(mine, "neuron").reshape(2 * rows, rank_width)
    ranks = spread(ranks, "trial")
    rank_g = ranks[:, :rows].reshape(-1, rank_width)
    rank_k = ranks[:, rows:].reshape(-1, rank_width)

    def by_stored(values):
        pieces = values.reshape(rows, trial_shards, stored).transpose(1, 0, 2)
        return swap(pieces, "trial").reshape(-1, stored)

    signal_mine = by_stored(signal_all)
    presyn_mine = by_stored(presyn_all)
    offset = lax.axis_index("trial") * stored
    left_rows = lax.dynamic_slice_in_dim(left_factor, offset, stored, 0).astype(jnp.float32)
    right_rows = lax.dynamic_slice_in_dim(right_factor, offset, stored, 0).astype(jnp.float32)
    lead = (((0,), (0,)), ((), ()))
    first = lax.dot_general(signal_mine, rank_g, lead, preferred_element_type=jnp.float32)
    second = lax.dot_general(presyn_mine, rank_k, lead, preferred_element_type=jnp.float32)
    left_step = left_rows - learn_rate * (first * norm_rank)
    right_step = right_rows - learn_rate * (second * norm_rank)
    highest = lax.Precision.HIGHEST
    gram_part = lax.dot_general(right_step, right_step, lead, precision=highest)
    everyone = ("neuron", "trial")
    gram_mine = jnp.sum(
        swap(gram_part.reshape(neuron_shards * trial_shards, -1, rank_width), everyone), 0
    )
    gram_one = spread(gram_mine, everyone).reshape(rank_width, rank_width)
    lower_one = jnp.linalg.cholesky(gram_one)
    basis = lax.linalg.triangular_solve(
        lower_one, right_step, left_side=False, lower=True, transpose_a=True
    )
    right_new = (basis * math.sqrt(neuron_count)).astype(jnp.bfloat16)
    left_new = (jnp.dot(left_step, lower_one, precision=highest) * norm_neurons).astype(
        jnp.bfloat16
    )
    return (left_new, right_new)


def solution(mesh):
    in_specs = (
        P(None, "trial", "neuron"),
        P(None, "trial", "neuron"),
        P("trial", "neuron"),
        P("trial", "neuron"),
        P("trial", "neuron"),
        P("neuron"),
        P("neuron"),
        P("neuron"),
        P("neuron"),
        P("neuron", None),
        P("neuron", None),
    )
    out_specs = (P(("neuron", "trial"), None), P(("neuron", "trial"), None))
    return jax.shard_map(shards, mesh=mesh, in_specs=in_specs, out_specs=out_specs, check_vma=False)
```

```python
import math

import jax
import jax.numpy as jnp
from jax import lax
from jax.experimental import pallas as pl
from jax.experimental.pallas import tpu as pltpu
from jax.sharding import PartitionSpec as P

sharpness = 3.0
learn_rate = 0.5

f32 = jnp.float32
bf16 = jnp.bfloat16
highest = lax.Precision.HIGHEST
block = 128

NN = (((1,), (0,)), ((), ()))
NT = (((1,), (1,)), ((), ()))
TN = (((0,), (0,)), ((), ()))

vmem = pl.BlockSpec(memory_space=pltpu.VMEM)


def dot(a, b, dims, precision=None):
    return lax.dot_general(a, b, dims, precision=precision, preferred_element_type=f32)


def swap(values, axes):
    return lax.all_to_all(values, axes, split_axis=0, concat_axis=0, tiled=True)


def spread(values, axes):
    copies = math.prod(lax.axis_size(a) for a in ((axes,) if isinstance(axes, str) else axes))
    return swap(jnp.broadcast_to(values[None], (copies,) + values.shape), axes)


def fire(membrane, adaptation, gain, threshold):
    level = membrane - threshold - gain * adaptation
    return 0.5 * jnp.tanh((0.5 * sharpness) * level) + 0.5


def post(total, weight, out_ref):
    total = (total * weight).astype(bf16)
    for i in range(out_ref.shape[0]):
        out_ref[i] = total


def halves(value):
    high = value.astype(bf16)
    return high, (value - high.astype(f32)).astype(bf16)


def dot3(a, b, dims):
    return dot(a[0], b[0], dims) + (dot(a[0], b[1], dims) + dot(a[1], b[0], dims))


def fetch(src_ref, dst_ref, sems, pieces):
    rows = src_ref.shape[0] // pieces
    copies = [
        pltpu.make_async_copy(
            src_ref.at[pl.ds(c * rows, rows)], dst_ref.at[pl.ds(c * rows, rows)], sems.at[c]
        )
        for c in range(pieces)
    ]
    for copy in copies:
        copy.start()
    return copies


def start_kernel(
    weight, me_ref, gain_ref, thr_ref, mem_ref, ada_ref, right_hbm, drive_hbm, learn_hbm,
    spk_ref, out_ref, right_ref, drive_ref, learn_ref, sems, sems_more,
):
    total = None
    copies = fetch(right_hbm, right_ref, sems, 8)
    more = fetch(drive_hbm, drive_ref, sems_more.at[0], 1)
    more += fetch(learn_hbm, learn_ref, sems_more.at[1], 1)
    width = right_ref.shape[0] // 8
    for c in range(8):
        at = pl.ds(c * width, width)
        spikes = fire(mem_ref[:, at], ada_ref[:, at], gain_ref[:, at], thr_ref[:, at])
        spk_ref[:, at] = spikes
        copies[c].wait()
        part = dot(spikes.astype(bf16), right_ref[at, :], NN)
        total = part if total is None else total + part
    post(total, weight, out_ref)
    for copy in more:
        copy.wait()


def step_kernel(weight_n, weight_r, moment, steps, *refs):
    first, last = moment == 0, moment + 1 == steps
    (me_ref, in_ref, dec_ref, ad_ref, gain_ref, thr_ref, drive_ref, learn_ref, mem_ref, ada_ref, fil_ref,
     spk_ref, left_ref, right_ref, sig_ref, pre_ref) = refs[:16]
    if not last:
        mem_out, ada_out, fil_out, spk_out, out_ref = refs[16:21]
    pieces, trials, width = sig_ref.shape
    if first:
        left_hbm, left_ref = left_ref, refs[21]
        copies = fetch(left_hbm, left_ref, refs[22], pieces)
    projected = jnp.sum(in_ref[...].astype(f32), 0).astype(bf16)
    total = None
    for c in range(pieces):
        at = pl.ds(c * width, width)
        decay, threshold = dec_ref[:, at], thr_ref[:, at]
        if first:
            copies[c].wait()
        current = dot(projected, left_ref[at, :], NT) * weight_r
        spikes = spk_ref[:, at]
        drive = drive_ref[moment, :, at].astype(f32)
        membrane = decay * mem_ref[:, at] + drive + current - threshold * spikes
        adaptation = ad_ref[:, at] * ada_ref[:, at] + spikes
        spikes = fire(membrane, adaptation, gain_ref[:, at], threshold)
        slope = sharpness * spikes * (1.0 - spikes)
        filtered = decay * fil_ref[:, at] + spikes
        slot = me_ref[0] ^ c
        sig_ref[slot] = (learn_ref[moment, :, at].astype(f32) * slope).astype(bf16)
        pre_ref[slot] = filtered.astype(bf16)
        if not last:
            mem_out[:, at] = membrane
            ada_out[:, at] = adaptation
            fil_out[:, at] = filtered
            spk_out[:, at] = spikes
            part = dot(spikes.astype(bf16), right_ref[at, :], NN)
            total = part if total is None else total + part
    if not last:
        post(total, weight_n, out_ref)


def ranks_kernel(weight, steps, me_ref, left_ref, right_ref, *refs):
    sigs, pres, outs = refs[:steps], refs[steps : 2 * steps], refs[2 * steps : -3]
    sig_held, pre_held, sems = refs[-3:]
    slots, trials, width = sigs[0].shape
    part_ref, sig_outs, pre_outs = outs[0], outs[1 : 1 + slots], outs[1 + slots :]
    copies = []
    for i, (values, held, results) in enumerate(
        ((pres, pre_held, pre_outs), (sigs, sig_held, sig_outs))
    ):
        for s in range(slots):
            for t, v in enumerate(values):
                held[s, t * trials : (t + 1) * trials] = v[s]
            copy = pltpu.make_async_copy(held.at[s], results[s], sems.at[i, s])
            copy.start()
            copies.append(copy)
    g = k = None
    for s in range(slots):
        at = pl.ds(pl.multiple_of((me_ref[0] ^ s) * width, width), width)
        a, b = dot(pre_held[s], right_ref[at, :], NN), dot(sig_held[s], left_ref[at, :], NN)
        g, k = (a, b) if g is None else (g + a, k + b)
    chunk = part_ref.shape[1]
    half = g.shape[0] // chunk
    for i in range(half):
        part_ref[i] = (g[i * chunk : (i + 1) * chunk] * weight).astype(bf16)
        part_ref[half + i] = (k[i * chunk : (i + 1) * chunk] * weight).astype(bf16)
    for copy in copies:
        copy.wait()


def again_kernel(in_ref, out_ref):
    total = jnp.sum(in_ref[...].astype(f32), 0).astype(out_ref.dtype)
    for i in range(out_ref.shape[0]):
        out_ref[i] = total


def update_kernel(weight, slots, me_ref, factor_hbm, *refs):
    ranks, pieces, outs, (rows, near, held, high, low, sem, sems, out_sem) = (
        refs[:slots], refs[slots : 2 * slots], refs[2 * slots : -8], refs[-8:]
    )
    me = me_ref[0]
    width, n = rows.shape
    copies = []
    for s in range(slots):
        for i, (src, dst) in enumerate(((ranks[s], near.at[s]), (pieces[s], held.at[s]))):
            copies.append(pltpu.make_async_copy(src, dst, sems.at[i, s]))
    own = pltpu.make_async_copy(
        factor_hbm.at[pl.ds(pl.multiple_of(me * width, width), width)], rows, sem
    )
    for copy in copies:
        copy.start()
    own.start()
    total = None
    for s in range(slots):
        copies[2 * s].wait()
        copies[2 * s + 1].wait()
        part = dot(held[s], near[s], TN)
        total = part if total is None else total + part
    own.wait()
    step = rows[...].astype(f32) - weight * total
    high[...], low[...] = halves(step)
    back = [
        pltpu.make_async_copy(v, outs[i], out_sem.at[i]) for i, v in enumerate((high, low))
    ]
    for copy in back:
        copy.start()
    if len(outs) > 2:
        square = dot(step, step, TN, highest)
        count, deep, wide = outs[2].shape
        across = n // wide
        for i in range(count):
            r, c = i // across, i % across
            outs[2][i] = square[r * deep : (r + 1) * deep, c * wide : (c + 1) * wide]
    for copy in back:
        copy.wait()


def diagonal(rows):
    groups = len(rows)
    lane = lax.broadcasted_iota(jnp.int32, (8, block), 1)
    sub = lax.broadcasted_iota(jnp.int32, (8, block), 0)
    wide = (8, block)
    rows = list(rows)
    ones = [jnp.where(lane == sub + 8 * g, 1.0, 0.0).astype(f32) for g in range(groups)]
    for g in range(groups):
        cols = [jnp.broadcast_to(rows[g][:, 8 * g + k : 8 * g + k + 1], wide) for k in range(8)]
        pivots = []
        a, e = rows[g], ones[g]
        for j in range(8):
            r = lax.rsqrt(jnp.broadcast_to(cols[j][j : j + 1, :], wide))
            m = jnp.where(sub > j, cols[j] * r, 0.0)
            us = [None] * 8
            for k in range(j + 1, 8):
                us[k] = jnp.broadcast_to(cols[k][j : j + 1, :], wide) * r
                cols[k] = cols[k] - m * us[k]
            ua = jnp.broadcast_to(a[j : j + 1, :], wide) * r
            ue = jnp.broadcast_to(e[j : j + 1, :], wide) * r
            a = jnp.where(sub == j, ua, a - m * ua)
            e = jnp.where(sub == j, ue, e - m * ue)
            pivots.append((r, us, ua, ue))
        rows[g], ones[g] = a, e
        for h in range(g + 1, groups):
            cols = [jnp.broadcast_to(rows[h][:, 8 * g + k : 8 * g + k + 1], wide) for k in range(8)]
            a, e = rows[h], ones[h]
            for j in range(8):
                r, us, ua, ue = pivots[j]
                m = cols[j] * r
                for k in range(j + 1, 8):
                    cols[k] = cols[k] - m * us[k]
                a = a - m * ua
                e = e - m * ue
            rows[h], ones[h] = a, e
    return ones


def finish_kernel(weight_l, weight_r, gram_ref, lh, ll, rh, rl, left_ref, right_ref, aug, part, steps, sems):
    n = left_ref.shape[1]
    blocks = n // block
    copies = [pltpu.make_async_copy(v, steps.at[i], sems.at[i]) for i, v in enumerate((lh, ll, rh, rl))]
    for copy in copies:
        copy.start()
    row = lax.broadcasted_iota(jnp.int32, (n, n), 0)
    col = lax.broadcasted_iota(jnp.int32, (n, n), 1)
    count, deep, wide = gram_ref.shape
    across = n // wide
    for i in range(count):
        r, c = i // across, i % across
        aug[r * deep : (r + 1) * deep, c * wide : (c + 1) * wide] = gram_ref[i]
    aug[:, n:] = jnp.where(row == col, 1.0, 0.0).astype(f32)

    def panel(p, carry):
        o = pl.multiple_of(p * block, block)
        ones = diagonal(
            [
                aug[pl.ds(pl.multiple_of(o + 8 * g, 8), 8), pl.ds(o, block)]
                for g in range(block // 8)
            ]
        )
        for g in range(block // 8):
            part[8 * g : 8 * g + 8, :] = ones[g]
        for k in range(blocks):

            @pl.when(p == k)
            def _(k=k):
                lo = k * block
                new = dot(part[...], aug[lo : lo + block, lo : n + lo + block], NN, highest)
                aug[lo : lo + block, lo : n + lo + block] = new
                if k + 1 < blocks:
                    aug[lo + block :, lo + block : n + lo + block] -= dot(
                        new[:, block : n - lo], new[:, block:], TN, highest
                    )

        return carry

    lax.fori_loop(0, blocks, panel, 0)
    upper = halves(jnp.where(row <= col, aug[:, :n], 0.0))
    inverse = halves(jnp.where(row >= col, aug[:, n:], 0.0))
    for copy in copies:
        copy.wait()
    rows = left_ref.shape[0] // 4
    for c in range(4):
        at = pl.ds(c * rows, rows)
        left_ref[at] = (dot3((steps[0, at], steps[1, at]), upper, NT) * weight_l).astype(bf16)
        right_ref[at] = (dot3((steps[2, at], steps[3, at]), inverse, NT) * weight_r).astype(bf16)


def call(kernel, args, outs, name, limit, scratch=(), aliases=None, far=(), far_outs=()):
    hbm = pl.BlockSpec(memory_space=pltpu.HBM)
    smem = pl.BlockSpec(memory_space=pltpu.SMEM)
    args = [
        pltpu.with_memory_space_constraint(a, pltpu.HBM) if i in far else a
        for i, a in enumerate(args)
    ]
    outs = [
        pltpu.HBM(o.shape, o.dtype) if i in far_outs else o for i, o in enumerate(outs)
    ]
    return pl.pallas_call(
        kernel,
        out_shape=outs,
        in_specs=[
            smem if a.dtype == jnp.int32 else hbm if i in far else vmem for i, a in enumerate(args)
        ],
        out_specs=[hbm if i in far_outs else vmem for i in range(len(outs))],
        scratch_shapes=scratch,
        input_output_aliases=aliases or {},
        name=name,
        compiler_params=pltpu.CompilerParams(vmem_limit_bytes=limit << 20),
    )(*args)


def shards(
    drive,
    learning,
    membrane_init,
    adapt_init,
    trace_init,
    membrane_decay,
    adapt_decay,
    adapt_gain,
    threshold,
    left_factor,
    right_factor,
):
    local_neurons, rank_width = left_factor.shape
    step_count, local_trials = drive.shape[:2]
    neuron_shards = lax.axis_size("neuron")
    trial_shards = lax.axis_size("trial")
    neuron_count = local_neurons * neuron_shards
    norm_neurons = 1.0 / math.sqrt(neuron_count)
    norm_rank = 1.0 / math.sqrt(rank_width)
    stored = local_neurons // trial_shards
    struct = jax.ShapeDtypeStruct
    decay, adecay, gain, level = (
        v.reshape(1, -1) for v in (membrane_decay, adapt_decay, adapt_gain, threshold)
    )
    state = pltpu.VMEM(membrane_init.shape, f32)
    sent = struct((neuron_shards, local_trials, rank_width), bf16)
    rows = step_count * local_trials
    slots = trial_shards
    everyone = ("neuron", "trial")
    me = lax.axis_index("trial").astype(jnp.int32).reshape(1)
    copy_sem = pltpu.SemaphoreType.DMA

    spikes, out, right_near, drive_near, learn_near = call(
        lambda *r: start_kernel(norm_neurons, *r),
        (me, gain, level, membrane_init, adapt_init, right_factor, drive, learning),
        [
            state,
            sent,
            pltpu.VMEM(right_factor.shape, bf16),
            pltpu.VMEM(drive.shape, bf16),
            pltpu.VMEM(learning.shape, bf16),
        ],
        "start",
        8,
        (copy_sem((8,)), copy_sem((2, 1))),
        far=(5, 6, 7),
    )
    states = [membrane_init, adapt_init, trace_init, spikes]
    held = struct((slots, local_trials, stored), bf16)
    left_near = left_factor
    signals = []
    presyns = []

    def exchange(values, k):
        return lax.ppermute(values, "trial", [(i, i ^ k) for i in range(slots)]) if k else values

    for moment in range(step_count):
        first, last = moment == 0, moment + 1 == step_count
        got = swap(out, "neuron")
        result = call(
            lambda *r, moment=moment: step_kernel(norm_neurons, norm_rank, moment, step_count, *r),
            (me, got, decay, adecay, gain, level, drive_near, learn_near, *states, left_near, right_near),
            [held, held]
            + ([] if last else [state, state, state, state, sent])
            + ([pltpu.VMEM(left_factor.shape, bf16)] if first else []),
            "step",
            8,
            (copy_sem((slots,)),) if first else (),
            {} if first or last else {8 + i: 2 + i for i in range(4)},
            (12,) if first else (),
        )
        signals.append(result[0])
        presyns.append(result[1])
        if not last:
            states, out = result[2:6], result[6]
        if first:
            left_near = result[7]

    chunk = 2 * rows // neuron_shards
    slot = struct((rows, stored), bf16)
    part, *pieces = call(
        lambda *r: ranks_kernel(norm_neurons, step_count, *r),
        (me, left_near, right_near, *signals, *presyns),
        [struct((neuron_shards, chunk, rank_width), bf16)] + [slot] * (2 * slots),
        "ranks",
        24,
        (
            pltpu.VMEM((slots, rows, stored), bf16),
            pltpu.VMEM((slots, rows, stored), bf16),
            copy_sem((2, slots)),
        ),
        far_outs=tuple(range(1, 1 + 2 * slots)),
    )
    presyn_mine = [exchange(v, k) for k, v in enumerate(pieces[slots:])]

    def again(blocks, copies):
        return call(
            again_kernel,
            (blocks,),
            [struct((copies,) + blocks.shape[1:], blocks.dtype)],
            "again",
            8,
        )[0]

    def everywhere(values):
        same = [exchange(values, 2 * j) for j in range(slots // 2)]
        return [v for s in same for v in (s, exchange(s, 1))]

    ranks = swap(again(swap(part, "neuron"), neuron_shards), "neuron")
    ranks = ranks.reshape(2, rows, rank_width)
    pair = struct((stored, rank_width), bf16)
    blocks = struct((neuron_shards * slots, 8, rank_width * rank_width // (8 * neuron_shards * slots)), f32)
    weight = learn_rate * norm_rank

    def update(factor, rank, values, gram):
        return call(
            lambda *r: update_kernel(weight, slots, *r),
            (me, factor, *rank, *values),
            [pair, pair] + ([blocks] if gram else []),
            "update",
            32,
            (
                pltpu.VMEM((stored, rank_width), bf16),
                pltpu.VMEM((slots, rows, rank_width), bf16),
                pltpu.VMEM((slots, rows, stored), bf16),
                pltpu.VMEM((stored, rank_width), bf16),
                pltpu.VMEM((stored, rank_width), bf16),
                copy_sem,
                copy_sem((2, slots)),
                copy_sem((2,)),
            ),
            far=tuple(range(1, 2 + 2 * slots)),
            far_outs=(0, 1),
        )

    right_hi, right_lo, gram_part = update(right_factor, everywhere(ranks[1]), presyn_mine, True)
    gram_part, rank_g, *late = lax.optimization_barrier((gram_part, ranks[0], *pieces[:slots]))
    rank_g = everywhere(rank_g)
    signal_mine = [exchange(v, k) for k, v in enumerate(late)]
    gram_one = swap(again(swap(gram_part, everyone), neuron_shards * slots), everyone)
    left_hi, left_lo = update(left_factor, rank_g, signal_mine, False)
    return tuple(
        call(
            lambda *r: finish_kernel(norm_neurons, math.sqrt(neuron_count), *r),
            (gram_one, left_hi, left_lo, right_hi, right_lo),
            [pair, pair],
            "finish",
            24,
            (
                pltpu.VMEM((rank_width, 2 * rank_width), f32),
                pltpu.VMEM((block, block), f32),
                pltpu.VMEM((4, stored, rank_width), bf16),
                copy_sem((4,)),
            ),
            far=(1, 2, 3, 4),
        )
    )


def solution(mesh):
    in_specs = (
        P(None, "trial", "neuron"),
        P(None, "trial", "neuron"),
        P("trial", "neuron"),
        P("trial", "neuron"),
        P("trial", "neuron"),
        P("neuron"),
        P("neuron"),
        P("neuron"),
        P("neuron"),
        P("neuron", None),
        P("neuron", None),
    )
    out_specs = (P(("neuron", "trial"), None), P(("neuron", "trial"), None))
    return jax.shard_map(shards, mesh=mesh, in_specs=in_specs, out_specs=out_specs, check_vma=False)
```

```python
import math

import jax
import jax.numpy as jnp
from jax import lax
from jax.experimental import pallas as pl
from jax.experimental.pallas import tpu as pltpu
from jax.sharding import PartitionSpec as P

sharpness = 3.0
learn_rate = 0.5

f32 = jnp.float32
bf16 = jnp.bfloat16
highest = lax.Precision.HIGHEST
block = 128
loops = 2

NN = (((1,), (0,)), ((), ()))
NT = (((1,), (1,)), ((), ()))
TN = (((0,), (0,)), ((), ()))

vmem = pl.BlockSpec(memory_space=pltpu.VMEM)


def dot(a, b, dims, precision=None):
    return lax.dot_general(a, b, dims, precision=precision, preferred_element_type=f32)


def swap(values, axes):
    return lax.all_to_all(values, axes, split_axis=0, concat_axis=0, tiled=True)


def spread(values, axes):
    copies = math.prod(lax.axis_size(a) for a in ((axes,) if isinstance(axes, str) else axes))
    return swap(jnp.broadcast_to(values[None], (copies,) + values.shape), axes)


def fire(membrane, adaptation, gain, threshold):
    level = membrane - threshold - gain * adaptation
    return 0.5 * jnp.tanh((0.5 * sharpness) * level) + 0.5


def post(total, weight, out_ref):
    total = (total * weight).astype(bf16)
    for i in range(out_ref.shape[0]):
        out_ref[i] = total


def halves(value):
    high = value.astype(bf16)
    return high, (value - high.astype(f32)).astype(bf16)


def dot3(a, b, dims):
    return dot(a[0], b[0], dims) + (dot(a[0], b[1], dims) + dot(a[1], b[0], dims))


def fetch(src_ref, dst_ref, sems, pieces):
    rows = src_ref.shape[0] // pieces
    copies = [
        pltpu.make_async_copy(
            src_ref.at[pl.ds(c * rows, rows)], dst_ref.at[pl.ds(c * rows, rows)], sems.at[c]
        )
        for c in range(pieces)
    ]
    for copy in copies:
        copy.start()
    return copies


def start_kernel(
    weight, me_ref, gain_hbm, thr_hbm, mem_hbm, ada_hbm, right_hbm, drive_hbm, learn_hbm,
    spk_ref, out_ref, right_ref, drive_ref, learn_ref, gain_ref, thr_ref, mem_ref, ada_ref, sems, sems_more,
):
    total = None
    pairs = (
        (gain_hbm, gain_ref), (thr_hbm, thr_ref), (mem_hbm, mem_ref), (ada_hbm, ada_ref),
        (drive_hbm, drive_ref), (learn_hbm, learn_ref),
    )
    more = [pltpu.make_async_copy(s, d, sems_more.at[i]) for i, (s, d) in enumerate(pairs)]
    for copy in more[:4]:
        copy.start()
    copies = fetch(right_hbm, right_ref, sems, 8)
    for copy in more[4:]:
        copy.start()
    for copy in more[:4]:
        copy.wait()
    width = right_ref.shape[0] // 8
    for c in range(8):
        at = pl.ds(c * width, width)
        spikes = fire(mem_ref[:, at], ada_ref[:, at], gain_ref[:, at], thr_ref[:, at])
        spk_ref[:, at] = spikes
        copies[c].wait()
        part = dot(spikes.astype(bf16), right_ref[at, :], NN)
        total = part if total is None else total + part
    post(total, weight, out_ref)
    for copy in more[4:]:
        copy.wait()


def step_kernel(weight_n, weight_r, moment, steps, *refs):
    first, last = moment == 0, moment + 1 == steps
    (me_ref, in_ref, dec_ref, ad_ref, gain_ref, thr_ref, drive_ref, learn_ref, mem_ref, ada_ref, fil_ref,
     spk_ref, left_ref, right_ref, sig_ref, pre_ref) = refs[:16]
    if not last:
        mem_out, ada_out, fil_out, spk_out, out_ref = refs[16:21]
    pieces, trials, width = sig_ref.shape
    if first:
        left_hbm, left_ref = left_ref, refs[21]
        copies = fetch(left_hbm, left_ref, refs[22], pieces)
    projected = jnp.sum(in_ref[...].astype(f32), 0).astype(bf16)

    def piece(c, total):
        at = pl.ds(pl.multiple_of(c * width, width), width)
        decay, threshold = dec_ref[:, at], thr_ref[:, at]
        current = dot(projected, left_ref[at, :], NT) * weight_r
        spikes = spk_ref[:, at]
        drive = drive_ref[moment, :, at].astype(f32)
        membrane = decay * mem_ref[:, at] + drive + current - threshold * spikes
        adaptation = ad_ref[:, at] * ada_ref[:, at] + spikes
        spikes = fire(membrane, adaptation, gain_ref[:, at], threshold)
        slope = sharpness * spikes * (1.0 - spikes)
        filtered = decay * fil_ref[:, at] + spikes
        slot = me_ref[0] ^ c
        sig_ref[c] = (learn_ref[moment, :, at].astype(f32) * slope).astype(bf16)
        pre_ref[slot] = filtered.astype(bf16)
        if last:
            return total
        mem_out[:, at] = membrane
        ada_out[:, at] = adaptation
        fil_out[:, at] = filtered
        spk_out[:, at] = spikes
        return total + dot(spikes.astype(bf16), right_ref[at, :], NN)

    total = jnp.zeros((trials, right_ref.shape[1]), f32)
    if first:
        for c in range(pieces):
            copies[c].wait()
            total = piece(c, total)
    else:

        def several(i, total):
            for c in range(pieces // loops):
                total = piece(i * (pieces // loops) + c, total)
            return total

        total = lax.fori_loop(0, loops, several, total)
    if not last:
        post(total, weight_n, out_ref)


def ranks_kernel(weight, steps, me_ref, left_ref, right_ref, *refs):
    sigs, pres, outs = refs[:steps], refs[steps : 2 * steps], refs[2 * steps : -3]
    sig_held, pre_held, sems = refs[-3:]
    slots, trials, width = sigs[0].shape
    part_ref, sig_out, pre_outs = outs[0], outs[1], outs[2:]
    sig_outs = [sig_out.at[s] for s in range(slots)]

    def gather(s, carry):
        for values, held in ((pres, pre_held), (sigs, sig_held)):
            for t, v in enumerate(values):
                held[s, t * trials : (t + 1) * trials] = v[s]
        return carry

    lax.fori_loop(0, slots, gather, 0)
    copies = [
        pltpu.make_async_copy(held.at[s], results[s], sems.at[i, s])
        for i, (held, results) in enumerate(((pre_held, pre_outs), (sig_held, sig_outs)))
        for s in range(slots)
    ]
    for copy in copies:
        copy.start()
    g = k = None
    for s in range(slots):
        at = pl.ds(pl.multiple_of((me_ref[0] ^ s) * width, width), width)
        a = dot(pre_held[s], right_ref[at, :], NN)
        b = dot(sig_held[s], left_ref[s * width : (s + 1) * width, :], NN)
        g, k = (a, b) if g is None else (g + a, k + b)
    chunk = part_ref.shape[1]
    half = g.shape[0] // chunk
    for i in range(half):
        part_ref[i] = (g[i * chunk : (i + 1) * chunk] * weight).astype(bf16)
        part_ref[half + i] = (k[i * chunk : (i + 1) * chunk] * weight).astype(bf16)
    for copy in copies:
        copy.wait()


def again_kernel(in_ref, out_ref):
    total = jnp.sum(in_ref[...].astype(f32), 0).astype(out_ref.dtype)
    for i in range(out_ref.shape[0]):
        out_ref[i] = total


def gradient(weight, slots, me_ref, factor_hbm, ranks, pieces, rows, near, held, sem, sems):
    width, n = rows.shape
    deep = pieces[0].shape[0]
    copies = []
    for s in range(slots):
        at = pl.ds(s * deep, deep)
        for i, (src, dst) in enumerate(((ranks[s], near), (pieces[s], held))):
            copies.append(pltpu.make_async_copy(src, dst.at[at], sems.at[i, s]))
    own = pltpu.make_async_copy(
        factor_hbm.at[pl.ds(pl.multiple_of(me_ref[0] * width, width), width)], rows, sem
    )
    for copy in copies:
        copy.start()
    own.start()
    total = None
    some = slots // 2
    for h in range(2):
        for copy in copies[h * slots : (h + 1) * slots]:
            copy.wait()
        at = pl.ds(h * some * deep, some * deep)
        part = dot(held[at], near[at], TN)
        total = part if total is None else total + part
    own.wait()
    return rows[...].astype(f32) - weight * total


def packing(n):
    return [(o, n - block - o) for o in range(0, n // 2, block)]


def right_kernel(weight, slots, me_ref, factor_hbm, *refs):
    high_hbm, low_hbm, gram_ref = refs[2 * slots : 2 * slots + 3]
    rows, near, held, high, low, sem, sems, out_sem = refs[2 * slots + 3 :]
    step = gradient(
        weight, slots, me_ref, factor_hbm, refs[:slots], refs[slots : 2 * slots], rows, near, held, sem, sems
    )
    high[...], low[...] = halves(step)
    back = [
        pltpu.make_async_copy(v, o, out_sem.at[i])
        for i, (v, o) in enumerate(((high, high_hbm), (low, low_hbm)))
    ]
    for copy in back:
        copy.start()
    n = high.shape[1]
    for group in packing(n):
        packed = jnp.concatenate(
            [
                dot3(
                    (high[:, o : o + block], low[:, o : o + block]), (high[:, o:], low[:, o:]), TN
                )
                for o in group
            ],
            1,
        )
        at = group[0] // 2
        for i in range(block // 2):
            gram_ref[at + i] = packed[2 * i : 2 * i + 2]
    for copy in back:
        copy.wait()


def left_kernel(weight, weight_l, slots, me_ref, high_ref, low_ref, factor_hbm, *refs):
    ranks, signal_hbm, out_ref, (rows, near, held, sem, sems) = (
        refs[:slots], refs[slots], refs[slots + 1], refs[slots + 2 :]
    )
    pieces = [signal_hbm.at[me_ref[0] ^ s] for s in range(slots)]
    step = halves(
        gradient(weight, slots, me_ref, factor_hbm, ranks, pieces, rows, near, held, sem, sems)
    )
    out_ref[...] = (dot3(step, (high_ref[...], low_ref[...]), NT) * weight_l).astype(bf16)


def diagonal(rows):
    groups = len(rows)
    wide = (8, block)
    lane = lax.broadcasted_iota(jnp.int32, wide, 1)
    sub = lax.broadcasted_iota(jnp.int32, wide, 0)
    rows = list(rows)
    ones = [jnp.where(lane == sub + 8 * g, 1.0, 0.0).astype(f32) for g in range(groups)]
    for g in range(groups):
        cols = [jnp.broadcast_to(rows[g][:, 8 * g + k : 8 * g + k + 1], wide) for k in range(8)]
        pivots = []
        a, e, root = rows[g], ones[g], None
        for j in range(8):
            d = jnp.broadcast_to(cols[j][j : j + 1, :], wide)
            inverse = 1.0 / d
            col = jnp.where(sub > j, cols[j], 0.0)
            us = [None] * 8
            for k in range(j + 1, 8):
                us[k] = jnp.broadcast_to(cols[k][j : j + 1, :], wide)
                cols[k] = cols[k] - (col * us[k]) * inverse
            ua = jnp.broadcast_to(a[j : j + 1, :], wide)
            ue = jnp.broadcast_to(e[j : j + 1, :], wide)
            m = col * inverse
            a = a - m * ua
            e = e - m * ue
            r = lax.rsqrt(d)
            root = r if root is None else jnp.where(sub == j, r, root)
            pivots.append((inverse, us, ua, ue))
        ones[g] = e * root
        for h in range(g + 1, groups):
            cols = [jnp.broadcast_to(rows[h][:, 8 * g + k : 8 * g + k + 1], wide) for k in range(8)]
            a, e = rows[h], ones[h]
            for j in range(8):
                inverse, us, ua, ue = pivots[j]
                m = cols[j] * inverse
                for k in range(j + 1, 8):
                    cols[k] = cols[k] - m * us[k]
                a = a - m * ua
                e = e - m * ue
            rows[h], ones[h] = a, e
    return ones


def finish_kernel(weight_r, gram_ref, rh, rl, upper_hi, upper_lo, right_ref, aug, part, steps, sems):
    n = right_ref.shape[1]
    blocks = n // block
    copies = [pltpu.make_async_copy(v, steps.at[i], sems.at[i]) for i, v in enumerate((rh, rl))]
    for copy in copies:
        copy.start()
    row = lax.broadcasted_iota(jnp.int32, (n, n), 0)
    col = lax.broadcasted_iota(jnp.int32, (n, n), 1)
    for group in packing(n):
        for i in range(block // 2):
            pair, at = gram_ref[group[0] // 2 + i], 0
            for o in group:
                aug[o + 2 * i : o + 2 * i + 2, o:n] = pair[:, at : at + n - o]
                at += n - o
    aug[:, n:] = jnp.where(row == col, 1.0, 0.0).astype(f32)

    def panel(p, carry):
        o = pl.multiple_of(p * block, block)
        ones = diagonal(
            [
                aug[pl.ds(pl.multiple_of(o + 8 * g, 8), 8), pl.ds(o, block)]
                for g in range(block // 8)
            ]
        )
        for g in range(block // 8):
            part[8 * g : 8 * g + 8, :] = ones[g]
        for k in range(blocks):

            @pl.when(p == k)
            def _(k=k):
                lo = k * block
                new = dot(part[...], aug[lo : lo + block, lo : n + lo + block], NN, highest)
                aug[lo : lo + block, lo : n + lo + block] = new
                if k + 1 < blocks:
                    aug[lo + block :, lo + block : n + lo + block] -= dot(
                        new[:, block : n - lo], new[:, block:], TN, highest
                    )

        return carry

    lax.fori_loop(0, blocks, panel, 0)
    upper_hi[...], upper_lo[...] = halves(jnp.where(row <= col, aug[:, :n], 0.0))
    inverse = halves(jnp.where(row >= col, aug[:, n:], 0.0))
    for copy in copies:
        copy.wait()
    right_ref[...] = (dot3((steps[0], steps[1]), inverse, NT) * weight_r).astype(bf16)


def call(kernel, args, outs, name, limit, scratch=(), aliases=None, far=(), far_outs=(), flops=None):
    hbm = pl.BlockSpec(memory_space=pltpu.HBM)
    smem = pl.BlockSpec(memory_space=pltpu.SMEM)
    args = [
        pltpu.with_memory_space_constraint(a, pltpu.HBM) if i in far else a
        for i, a in enumerate(args)
    ]
    outs = [
        pltpu.HBM(o.shape, o.dtype) if i in far_outs else o for i, o in enumerate(outs)
    ]
    return pl.pallas_call(
        kernel,
        out_shape=outs,
        in_specs=[
            smem if a.dtype == jnp.int32 else hbm if i in far else vmem for i, a in enumerate(args)
        ],
        out_specs=[hbm if i in far_outs else vmem for i in range(len(outs))],
        scratch_shapes=scratch,
        input_output_aliases=aliases or {},
        name=name,
        cost_estimate=flops and pl.CostEstimate(flops=flops, transcendentals=0, bytes_accessed=0),
        compiler_params=pltpu.CompilerParams(vmem_limit_bytes=limit << 20),
    )(*args)


def shards(
    drive,
    learning,
    membrane_init,
    adapt_init,
    trace_init,
    membrane_decay,
    adapt_decay,
    adapt_gain,
    threshold,
    left_factor,
    right_factor,
):
    local_neurons, rank_width = left_factor.shape
    step_count, local_trials = drive.shape[:2]
    neuron_shards = lax.axis_size("neuron")
    trial_shards = lax.axis_size("trial")
    neuron_count = local_neurons * neuron_shards
    norm_neurons = 1.0 / math.sqrt(neuron_count)
    norm_rank = 1.0 / math.sqrt(rank_width)
    stored = local_neurons // trial_shards
    struct = jax.ShapeDtypeStruct
    decay, adecay, gain, level = (
        v.reshape(1, -1) for v in (membrane_decay, adapt_decay, adapt_gain, threshold)
    )
    state = pltpu.VMEM(membrane_init.shape, f32)
    sent = struct((neuron_shards, local_trials, rank_width), bf16)
    rows = step_count * local_trials
    slots = trial_shards
    everyone = ("neuron", "trial")
    me = lax.axis_index("trial").astype(jnp.int32).reshape(1)
    copy_sem = pltpu.SemaphoreType.DMA

    spikes, out, right_near, drive_near, learn_near = call(
        lambda *r: start_kernel(norm_neurons, *r),
        (me, gain, level, membrane_init, adapt_init, right_factor, drive, learning),
        [
            state,
            sent,
            pltpu.VMEM(right_factor.shape, bf16),
            pltpu.VMEM(drive.shape, bf16),
            pltpu.VMEM(learning.shape, bf16),
        ],
        "start",
        8,
        (
            pltpu.VMEM(gain.shape, f32),
            pltpu.VMEM(level.shape, f32),
            pltpu.VMEM(membrane_init.shape, f32),
            pltpu.VMEM(adapt_init.shape, f32),
            copy_sem((8,)),
            copy_sem((6,)),
        ),
        far=tuple(range(1, 8)),
    )
    states = [membrane_init, adapt_init, trace_init, spikes]
    held = struct((slots, local_trials, stored), bf16)
    left_near = left_factor
    signals = []
    presyns = []

    def exchange(values, k):
        return lax.ppermute(values, "trial", [(i, i ^ k) for i in range(slots)]) if k else values

    for moment in range(step_count):
        first, last = moment == 0, moment + 1 == step_count
        got = swap(out, "neuron")
        result = call(
            lambda *r, moment=moment: step_kernel(norm_neurons, norm_rank, moment, step_count, *r),
            (me, got, decay, adecay, gain, level, drive_near, learn_near, *states, left_near, right_near),
            [held, held]
            + ([] if last else [state, state, state, state, sent])
            + ([pltpu.VMEM(left_factor.shape, bf16)] if first else []),
            "step",
            8,
            (copy_sem((slots,)),) if first else (),
            {} if first or last else {8 + i: 2 + i for i in range(4)},
            (12,) if first else (),
        )
        signals.append(result[0])
        presyns.append(result[1])
        if not last:
            states, out = result[2:6], result[6]
        if first:
            left_near = result[7]

    chunk = 2 * rows // neuron_shards
    slot = struct((rows, stored), bf16)
    part, signal_all, *presyn_mine = call(
        lambda *r: ranks_kernel(norm_neurons, step_count, *r),
        (me, left_near, right_near, *signals, *presyns),
        [struct((neuron_shards, chunk, rank_width), bf16), struct((slots, rows, stored), bf16)]
        + [slot] * slots,
        "ranks",
        24,
        (
            pltpu.VMEM((slots, rows, stored), bf16),
            pltpu.VMEM((slots, rows, stored), bf16),
            copy_sem((2, slots)),
        ),
        far_outs=tuple(range(1, 2 + slots)),
    )
    down = [(i, (i - 2) % slots) for i in range(slots)]
    over = [(i, ((i - 2) % slots) ^ 1) for i in range(slots)]
    opposite = {4: exchange(presyn_mine[4], 4), 5: lax.ppermute(presyn_mine[5], "trial", down)}
    presyn_mine = [opposite[k] if k in opposite else exchange(v, k) for k, v in enumerate(presyn_mine)]

    def again(blocks, copies):
        return call(
            again_kernel,
            (blocks,),
            [struct((copies,) + blocks.shape[1:], blocks.dtype)],
            "again",
            8,
        )[0]

    def everywhere(values):
        same = [exchange(values, 2 * j) for j in range(slots // 2)]
        return [v for s in same for v in (s, exchange(s, 1))]

    mine = again(swap(part, "neuron"), neuron_shards)
    near = [4, 5, 2, 3]
    mine, *moved = lax.optimization_barrier((mine, *[presyn_mine[k] for k in near]))
    for k, v in zip(near, moved, strict=True):
        presyn_mine[k] = v
    presyn_mine[5] = lax.ppermute(presyn_mine[5], "trial", over)
    ranks = swap(mine, "neuron")
    ranks = ranks.reshape(2, rows, rank_width)
    pair = struct((stored, rank_width), bf16)
    blocks = struct((rank_width // 4, 2, rank_width + block), f32)
    weight = learn_rate * norm_rank

    far = 2 * slots + 1
    scratch = (
        pltpu.VMEM((stored, rank_width), bf16),
        pltpu.VMEM((slots * rows, rank_width), bf16),
        pltpu.VMEM((slots * rows, stored), bf16),
    )
    sems = (copy_sem, copy_sem((2, slots)))
    right_hi, right_lo, gram_part = call(
        lambda *r: right_kernel(weight, slots, *r),
        (me, right_factor, *everywhere(ranks[1]), *presyn_mine),
        [pair, pair, blocks],
        "right",
        32,
        (*scratch, *scratch[:1], *scratch[:1], *sems, copy_sem((2,))),
        far=tuple(range(1, 1 + far)),
        far_outs=(0, 1),
    )
    gram_part, rank_g = lax.optimization_barrier((gram_part, ranks[0]))
    rank_g = everywhere(rank_g)
    gram_one = swap(again(swap(gram_part, everyone), neuron_shards * slots), everyone)
    gram_one, signal_all = lax.optimization_barrier((gram_one, signal_all))
    signal_mine = swap(signal_all, "trial")
    square = struct((rank_width, rank_width), bf16)
    upper_hi, upper_lo, right_new = call(
        lambda *r: finish_kernel(math.sqrt(neuron_count), *r),
        (gram_one, right_hi, right_lo),
        [square, square, pair],
        "finish",
        24,
        (
            pltpu.VMEM((rank_width, 2 * rank_width), f32),
            pltpu.VMEM((block, block), f32),
            pltpu.VMEM((2, stored, rank_width), bf16),
            copy_sem((2,)),
        ),
        far=(1, 2),
        flops=20 * 10**9,
    )
    (left_new,) = call(
        lambda *r: left_kernel(weight, norm_neurons, slots, *r),
        (me, upper_hi, upper_lo, left_factor, *rank_g, signal_mine),
        [pair],
        "left",
        32,
        (*scratch, *sems),
        far=tuple(range(3, 5 + slots)),
    )
    return (left_new, right_new)


def solution(mesh):
    in_specs = (
        P(None, "trial", "neuron"),
        P(None, "trial", "neuron"),
        P("trial", "neuron"),
        P("trial", "neuron"),
        P("trial", "neuron"),
        P("neuron"),
        P("neuron"),
        P("neuron"),
        P("neuron"),
        P("neuron", None),
        P("neuron", None),
    )
    out_specs = (P(("neuron", "trial"), None), P(("neuron", "trial"), None))
    return jax.shard_map(shards, mesh=mesh, in_specs=in_specs, out_specs=out_specs, check_vma=False)
```

```python
import math

import jax
import jax.numpy as jnp
from jax import lax
from jax.experimental import pallas as pl
from jax.experimental.pallas import tpu as pltpu
from jax.sharding import PartitionSpec as P

sharpness = 3.0
learn_rate = 0.5

f32 = jnp.float32
bf16 = jnp.bfloat16
highest = lax.Precision.HIGHEST
block = 128
loops = 2

NN = (((1,), (0,)), ((), ()))
NT = (((1,), (1,)), ((), ()))
TN = (((0,), (0,)), ((), ()))

vmem = pl.BlockSpec(memory_space=pltpu.VMEM)


def dot(a, b, dims, precision=None):
    return lax.dot_general(a, b, dims, precision=precision, preferred_element_type=f32)


def swap(values, axes):
    return lax.all_to_all(values, axes, split_axis=0, concat_axis=0, tiled=True)


def spread(values, axes):
    copies = math.prod(lax.axis_size(a) for a in ((axes,) if isinstance(axes, str) else axes))
    return swap(jnp.broadcast_to(values[None], (copies,) + values.shape), axes)


def fire(membrane, adaptation, gain, threshold):
    level = membrane - threshold - gain * adaptation
    return 0.5 * jnp.tanh((0.5 * sharpness) * level) + 0.5


def post(total, weight, out_ref):
    total = (total * weight).astype(bf16)
    for i in range(out_ref.shape[0]):
        out_ref[i] = total


def halves(value):
    high = value.astype(bf16)
    return high, (value - high.astype(f32)).astype(bf16)


def dot3(a, b, dims):
    return dot(a[0], b[0], dims) + (dot(a[0], b[1], dims) + dot(a[1], b[0], dims))


def fetch(src_ref, dst_ref, sems, pieces):
    rows = src_ref.shape[0] // pieces
    copies = [
        pltpu.make_async_copy(
            src_ref.at[pl.ds(c * rows, rows)], dst_ref.at[pl.ds(c * rows, rows)], sems.at[c]
        )
        for c in range(pieces)
    ]
    for copy in copies:
        copy.start()
    return copies


def start_kernel(
    weight, me_ref, gain_hbm, thr_hbm, mem_hbm, ada_hbm, right_hbm, drive_hbm, learn_hbm,
    spk_ref, out_ref, right_ref, drive_ref, learn_ref, gain_ref, thr_ref, mem_ref, ada_ref, sems, sems_more,
):
    pairs = (
        (gain_hbm, gain_ref), (thr_hbm, thr_ref), (mem_hbm, mem_ref), (ada_hbm, ada_ref),
        (drive_hbm, drive_ref), (learn_hbm, learn_ref),
    )
    more = [pltpu.make_async_copy(s, d, sems_more.at[i]) for i, (s, d) in enumerate(pairs)]
    for copy in more[:4]:
        copy.start()
    copies = fetch(right_hbm, right_ref, sems, 8)
    for copy in more[4:]:
        copy.start()
    for copy in more[:4]:
        copy.wait()
    count = len(copies)
    width = right_ref.shape[0] // count

    def several(i, total):
        for c in range(2):
            c = 2 * i + c
            at = pl.ds(pl.multiple_of(c * width, width), width)
            spikes = fire(mem_ref[:, at], ada_ref[:, at], gain_ref[:, at], thr_ref[:, at])
            spk_ref[:, at] = spikes
            pltpu.make_async_copy(right_hbm.at[at], right_ref.at[at], sems.at[c]).wait()
            total = total + dot(spikes.astype(bf16), right_ref[at, :], NN)
        return total

    total = jnp.zeros((mem_ref.shape[0], right_ref.shape[1]), f32)
    post(lax.fori_loop(0, count // 2, several, total), weight, out_ref)
    for copy in more[4:]:
        copy.wait()


def step_kernel(weight_n, weight_r, moment, steps, *refs):
    first, last = moment == 0, moment + 1 == steps
    (me_ref, in_ref, dec_ref, ad_ref, gain_ref, thr_ref, drive_ref, learn_ref, mem_ref, ada_ref, fil_ref,
     spk_ref, left_ref, right_ref) = refs[:14]
    outs = refs[14:] if first else refs[16:]
    sig_ref, pre_ref = outs[:2]
    if not last:
        mem_out, ada_out, fil_out, spk_out, out_ref = outs[2:7]
    pieces, _, width = sig_ref.shape
    trials = mem_ref.shape[0]
    rows = pl.ds(moment * trials, trials)
    if first:
        left_hbm, left_ref = left_ref, outs[7]
        sems = outs[8]
        fetch(left_hbm, left_ref, sems, pieces)
    projected = jnp.sum(in_ref[...].astype(f32), 0).astype(bf16)

    def piece(c, total):
        at = pl.ds(pl.multiple_of(c * width, width), width)
        decay, threshold = dec_ref[:, at], thr_ref[:, at]
        if first:
            pltpu.make_async_copy(left_hbm.at[at], left_ref.at[at], sems.at[c]).wait()
        current = dot(projected, left_ref[at, :], NT) * weight_r
        spikes = spk_ref[:, at]
        drive = drive_ref[moment, :, at].astype(f32)
        membrane = decay * mem_ref[:, at] + drive + current - threshold * spikes
        adaptation = ad_ref[:, at] * ada_ref[:, at] + spikes
        spikes = fire(membrane, adaptation, gain_ref[:, at], threshold)
        slope = sharpness * spikes * (1.0 - spikes)
        filtered = decay * fil_ref[:, at] + spikes
        slot = me_ref[0] ^ c
        sig_ref[c, rows] = (learn_ref[moment, :, at].astype(f32) * slope).astype(bf16)
        pre_ref[slot, rows] = filtered.astype(bf16)
        if last:
            return total
        mem_out[:, at] = membrane
        ada_out[:, at] = adaptation
        fil_out[:, at] = filtered
        spk_out[:, at] = spikes
        return total + dot(spikes.astype(bf16), right_ref[at, :], NN)

    total = jnp.zeros((trials, right_ref.shape[1]), f32)

    def several(i, total):
        for c in range(pieces // loops):
            total = piece(i * (pieces // loops) + c, total)
        return total

    total = lax.fori_loop(0, loops, several, total)
    if not last:
        post(total, weight_n, out_ref)


def ranks_kernel(weight, me_ref, left_ref, right_ref, sig_ref, pre_ref, part_ref, sig_out, *refs):
    pre_outs, sems = refs[:-1], refs[-1]
    slots, _, width = sig_ref.shape
    copies = [
        pltpu.make_async_copy(pre_ref.at[s], o, sems.at[s]) for s, o in enumerate(pre_outs)
    ]
    copies.append(pltpu.make_async_copy(sig_ref, sig_out, sems.at[slots]))
    for copy in copies:
        copy.start()
    g = k = None
    for s in range(slots):
        at = pl.ds(pl.multiple_of((me_ref[0] ^ s) * width, width), width)
        a = dot(pre_ref[s], right_ref[at, :], NN)
        b = dot(sig_ref[s], left_ref[s * width : (s + 1) * width, :], NN)
        g, k = (a, b) if g is None else (g + a, k + b)
    chunk = part_ref.shape[1]
    half = g.shape[0] // chunk
    for i in range(half):
        part_ref[i] = (g[i * chunk : (i + 1) * chunk] * weight).astype(bf16)
        part_ref[half + i] = (k[i * chunk : (i + 1) * chunk] * weight).astype(bf16)
    for copy in copies:
        copy.wait()


def again_kernel(in_ref, out_ref):
    total = jnp.sum(in_ref[...].astype(f32), 0).astype(out_ref.dtype)
    for i in range(out_ref.shape[0]):
        out_ref[i] = total


def gradient(weight, slots, me_ref, factor_hbm, ranks, pieces, rows, near, held, sem, sems, use):
    width = rows.shape[0]
    deep = pieces[0].shape[0]
    copies = []
    for s in range(slots):
        at = pl.ds(s * deep, deep)
        for i, (src, dst) in enumerate(((ranks[s], near), (pieces[s], held))):
            copies.append(pltpu.make_async_copy(src, dst.at[at], sems.at[i, s]))
    copies.append(
        pltpu.make_async_copy(
            factor_hbm.at[pl.ds(pl.multiple_of(me_ref[0] * width, width), width)], rows, sem
        )
    )
    for copy in copies:
        copy.start()
    for copy in copies:
        copy.wait()
    size = 4 * block

    def several(i, carry):
        at = pl.ds(pl.multiple_of(i * size, size), size)
        use(at, rows[at].astype(f32) - weight * dot(held[:, at], near[...], TN))
        return carry

    lax.fori_loop(0, width // size, several, 0)


def packing(n):
    return [(o, n - block - o) for o in range(0, n // 2, block)]


def right_kernel(weight, slots, me_ref, factor_hbm, *refs):
    high_hbm, low_hbm, gram_ref = refs[2 * slots : 2 * slots + 3]
    rows, near, held, high, low, sem, sems, out_sem = refs[2 * slots + 3 :]

    def use(at, step):
        high[at], low[at] = halves(step)

    gradient(
        weight, slots, me_ref, factor_hbm, refs[:slots], refs[slots : 2 * slots], rows, near, held, sem, sems, use
    )
    back = [
        pltpu.make_async_copy(v, o, out_sem.at[i])
        for i, (v, o) in enumerate(((high, high_hbm), (low, low_hbm)))
    ]
    for copy in back:
        copy.start()
    n = high.shape[1]
    for group in packing(n):
        packed = jnp.concatenate(
            [
                dot3(
                    (high[:, o : o + block], low[:, o : o + block]), (high[:, o:], low[:, o:]), TN
                )
                for o in group
            ],
            1,
        )
        at = group[0] // 2
        for i in range(block // 2):
            gram_ref[at + i] = packed[2 * i : 2 * i + 2]
    for copy in back:
        copy.wait()


def left_kernel(weight, weight_l, slots, me_ref, high_ref, low_ref, factor_hbm, *refs):
    ranks, signal_hbm, out_ref, (rows, near, held, sem, sems) = (
        refs[:slots], refs[slots], refs[slots + 1], refs[slots + 2 :]
    )
    pieces = [signal_hbm.at[me_ref[0] ^ s] for s in range(slots)]
    upper = high_ref[...], low_ref[...]

    def use(at, step):
        out_ref[at] = (dot3(halves(step), upper, NT) * weight_l).astype(bf16)

    gradient(weight, slots, me_ref, factor_hbm, ranks, pieces, rows, near, held, sem, sems, use)


def diagonal(rows):
    groups = len(rows)
    wide = (8, block)
    lane = lax.broadcasted_iota(jnp.int32, wide, 1)
    sub = lax.broadcasted_iota(jnp.int32, wide, 0)
    rows = list(rows)
    ones = [jnp.where(lane == sub + 8 * g, 1.0, 0.0).astype(f32) for g in range(groups)]
    for g in range(groups):
        cols = [jnp.broadcast_to(rows[g][:, 8 * g + k : 8 * g + k + 1], wide) for k in range(8)]
        pivots = []
        a, e, root = rows[g], ones[g], None
        for j in range(8):
            d = jnp.broadcast_to(cols[j][j : j + 1, :], wide)
            inverse = 1.0 / d
            col = jnp.where(sub > j, cols[j], 0.0)
            us = [None] * 8
            for k in range(j + 1, 8):
                us[k] = jnp.broadcast_to(cols[k][j : j + 1, :], wide)
                cols[k] = cols[k] - (col * us[k]) * inverse
            ua = jnp.broadcast_to(a[j : j + 1, :], wide)
            ue = jnp.broadcast_to(e[j : j + 1, :], wide)
            m = col * inverse
            a = a - m * ua
            e = e - m * ue
            r = lax.rsqrt(d)
            root = r if root is None else jnp.where(sub == j, r, root)
            pivots.append((inverse, us, ua, ue))
        ones[g] = e * root
        for h in range(g + 1, groups):
            cols = [jnp.broadcast_to(rows[h][:, 8 * g + k : 8 * g + k + 1], wide) for k in range(8)]
            a, e = rows[h], ones[h]
            for j in range(8):
                inverse, us, ua, ue = pivots[j]
                m = cols[j] * inverse
                for k in range(j + 1, 8):
                    cols[k] = cols[k] - m * us[k]
                a = a - m * ua
                e = e - m * ue
            rows[h], ones[h] = a, e
    return ones


def finish_kernel(weight_r, gram_ref, rh, rl, upper_hi, upper_lo, right_ref, aug, part, steps, sems):
    n = right_ref.shape[1]
    blocks = n // block
    copies = [pltpu.make_async_copy(v, steps.at[i], sems.at[i]) for i, v in enumerate((rh, rl))]
    for copy in copies:
        copy.start()
    row = lax.broadcasted_iota(jnp.int32, (n, n), 0)
    col = lax.broadcasted_iota(jnp.int32, (n, n), 1)
    for group in packing(n):
        for i in range(block // 2):
            pair, at = gram_ref[group[0] // 2 + i], 0
            for o in group:
                aug[o + 2 * i : o + 2 * i + 2, o:n] = pair[:, at : at + n - o]
                at += n - o
    aug[:, n:] = jnp.where(row == col, 1.0, 0.0).astype(f32)

    def panel(p, carry):
        o = pl.multiple_of(p * block, block)
        ones = diagonal(
            [
                aug[pl.ds(pl.multiple_of(o + 8 * g, 8), 8), pl.ds(o, block)]
                for g in range(block // 8)
            ]
        )
        for g in range(block // 8):
            part[8 * g : 8 * g + 8, :] = ones[g]
        for k in range(blocks):

            @pl.when(p == k)
            def _(k=k):
                lo = k * block
                new = dot(part[...], aug[lo : lo + block, lo : n + lo + block], NN, highest)
                aug[lo : lo + block, lo : n + lo + block] = new
                if k + 1 < blocks:
                    aug[lo + block :, lo + block : n + lo + block] -= dot(
                        new[:, block : n - lo], new[:, block:], TN, highest
                    )

        return carry

    lax.fori_loop(0, blocks, panel, 0)
    upper_hi[...], upper_lo[...] = halves(jnp.where(row <= col, aug[:, :n], 0.0))
    inverse = halves(jnp.where(row >= col, aug[:, n:], 0.0))
    for copy in copies:
        copy.wait()
    right_ref[...] = (dot3((steps[0], steps[1]), inverse, NT) * weight_r).astype(bf16)


def call(kernel, args, outs, name, limit, scratch=(), aliases=None, far=(), far_outs=(), flops=None):
    hbm = pl.BlockSpec(memory_space=pltpu.HBM)
    smem = pl.BlockSpec(memory_space=pltpu.SMEM)
    args = [
        pltpu.with_memory_space_constraint(a, pltpu.HBM) if i in far else a
        for i, a in enumerate(args)
    ]
    outs = [
        pltpu.HBM(o.shape, o.dtype) if i in far_outs else o for i, o in enumerate(outs)
    ]
    return pl.pallas_call(
        kernel,
        out_shape=outs,
        in_specs=[
            smem if a.dtype == jnp.int32 else hbm if i in far else vmem for i, a in enumerate(args)
        ],
        out_specs=[hbm if i in far_outs else vmem for i in range(len(outs))],
        scratch_shapes=scratch,
        input_output_aliases=aliases or {},
        name=name,
        cost_estimate=flops and pl.CostEstimate(flops=flops, transcendentals=0, bytes_accessed=0),
        compiler_params=pltpu.CompilerParams(vmem_limit_bytes=limit << 20),
    )(*args)


def shards(
    drive,
    learning,
    membrane_init,
    adapt_init,
    trace_init,
    membrane_decay,
    adapt_decay,
    adapt_gain,
    threshold,
    left_factor,
    right_factor,
):
    local_neurons, rank_width = left_factor.shape
    step_count, local_trials = drive.shape[:2]
    neuron_shards = lax.axis_size("neuron")
    trial_shards = lax.axis_size("trial")
    neuron_count = local_neurons * neuron_shards
    norm_neurons = 1.0 / math.sqrt(neuron_count)
    norm_rank = 1.0 / math.sqrt(rank_width)
    stored = local_neurons // trial_shards
    struct = jax.ShapeDtypeStruct
    decay, adecay, gain, level = (
        v.reshape(1, -1) for v in (membrane_decay, adapt_decay, adapt_gain, threshold)
    )
    state = pltpu.VMEM(membrane_init.shape, f32)
    sent = struct((neuron_shards, local_trials, rank_width), bf16)
    rows = step_count * local_trials
    slots = trial_shards
    everyone = ("neuron", "trial")
    me = lax.axis_index("trial").astype(jnp.int32).reshape(1)
    copy_sem = pltpu.SemaphoreType.DMA

    spikes, out, right_near, drive_near, learn_near = call(
        lambda *r: start_kernel(norm_neurons, *r),
        (me, gain, level, membrane_init, adapt_init, right_factor, drive, learning),
        [
            state,
            sent,
            pltpu.VMEM(right_factor.shape, bf16),
            pltpu.VMEM(drive.shape, bf16),
            pltpu.VMEM(learning.shape, bf16),
        ],
        "start",
        8,
        (
            pltpu.VMEM(gain.shape, f32),
            pltpu.VMEM(level.shape, f32),
            pltpu.VMEM(membrane_init.shape, f32),
            pltpu.VMEM(adapt_init.shape, f32),
            copy_sem((8,)),
            copy_sem((6,)),
        ),
        far=tuple(range(1, 8)),
    )
    states = [membrane_init, adapt_init, trace_init, spikes]
    kept = pltpu.VMEM((slots, rows, stored), bf16)
    left_near = left_factor
    every = ()

    def exchange(values, k):
        return lax.ppermute(values, "trial", [(i, i ^ k) for i in range(slots)]) if k else values

    for moment in range(step_count):
        first, last = moment == 0, moment + 1 == step_count
        got = swap(out, "neuron")
        result = call(
            lambda *r, moment=moment: step_kernel(norm_neurons, norm_rank, moment, step_count, *r),
            (me, got, decay, adecay, gain, level, drive_near, learn_near, *states, left_near, right_near, *every),
            [kept, kept]
            + ([] if last else [state, state, state, state, sent])
            + ([pltpu.VMEM(left_factor.shape, bf16)] if first else []),
            "step",
            8,
            (copy_sem((slots,)),) if first else (),
            {} if first else {14: 0, 15: 1} | ({} if last else {8 + i: 2 + i for i in range(4)}),
            (12,) if first else (),
        )
        every = result[:2]
        if not last:
            states, out = result[2:6], result[6]
        if first:
            left_near = result[7]

    chunk = 2 * rows // neuron_shards
    slot = struct((rows, stored), bf16)
    part, signal_all, *presyn_mine = call(
        lambda *r: ranks_kernel(norm_neurons, *r),
        (me, left_near, right_near, *every),
        [struct((neuron_shards, chunk, rank_width), bf16), struct((slots, rows, stored), bf16)]
        + [slot] * slots,
        "ranks",
        16,
        (copy_sem((slots + 1,)),),
        far_outs=tuple(range(1, 2 + slots)),
    )
    down = [(i, (i - 2) % slots) for i in range(slots)]
    over = [(i, ((i - 2) % slots) ^ 1) for i in range(slots)]
    opposite = {4: exchange(presyn_mine[4], 4), 5: lax.ppermute(presyn_mine[5], "trial", down)}
    presyn_mine = [opposite[k] if k in opposite else exchange(v, k) for k, v in enumerate(presyn_mine)]

    def again(blocks, copies):
        return call(
            again_kernel,
            (blocks,),
            [struct((copies,) + blocks.shape[1:], blocks.dtype)],
            "again",
            8,
        )[0]

    def everywhere(values):
        same = [exchange(values, 2 * j) for j in range(slots // 2)]
        return [v for s in same for v in (s, exchange(s, 1))]

    mine = again(swap(part, "neuron"), neuron_shards)
    near = [4, 5, 2, 3, 6]
    mine, *moved = lax.optimization_barrier((mine, *[presyn_mine[k] for k in near]))
    for k, v in zip(near, moved, strict=True):
        presyn_mine[k] = v
    presyn_mine[5] = lax.ppermute(presyn_mine[5], "trial", over)
    ranks = swap(mine, "neuron")
    ranks = ranks.reshape(2, rows, rank_width)
    pair = struct((stored, rank_width), bf16)
    blocks = struct((rank_width // 4, 2, rank_width + block), f32)
    weight = learn_rate * norm_rank

    far = 2 * slots + 1
    scratch = (
        pltpu.VMEM((stored, rank_width), bf16),
        pltpu.VMEM((slots * rows, rank_width), bf16),
        pltpu.VMEM((slots * rows, stored), bf16),
    )
    sems = (copy_sem, copy_sem((2, slots)))
    right_hi, right_lo, gram_part = call(
        lambda *r: right_kernel(weight, slots, *r),
        (me, right_factor, *everywhere(ranks[1]), *presyn_mine),
        [pair, pair, blocks],
        "right",
        32,
        (*scratch, *scratch[:1], *scratch[:1], *sems, copy_sem((2,))),
        far=tuple(range(1, 1 + far)),
        far_outs=(0, 1),
    )
    gram_part, rank_g = lax.optimization_barrier((gram_part, ranks[0]))
    rank_g = everywhere(rank_g)
    gram_one = swap(again(swap(gram_part, everyone), neuron_shards * slots), everyone)
    gram_one, signal_all = lax.optimization_barrier((gram_one, signal_all))
    signal_mine = swap(signal_all, "trial")
    square = struct((rank_width, rank_width), bf16)
    upper_hi, upper_lo, right_new = call(
        lambda *r: finish_kernel(math.sqrt(neuron_count), *r),
        (gram_one, right_hi, right_lo),
        [square, square, pair],
        "finish",
        24,
        (
            pltpu.VMEM((rank_width, 2 * rank_width), f32),
            pltpu.VMEM((block, block), f32),
            pltpu.VMEM((2, stored, rank_width), bf16),
            copy_sem((2,)),
        ),
        far=(1, 2),
        flops=20 * 10**9,
    )
    (left_new,) = call(
        lambda *r: left_kernel(weight, norm_neurons, slots, *r),
        (me, upper_hi, upper_lo, left_factor, *rank_g, signal_mine),
        [pair],
        "left",
        32,
        (*scratch, *sems),
        far=tuple(range(3, 5 + slots)),
    )
    return (left_new, right_new)


def solution(mesh):
    in_specs = (
        P(None, "trial", "neuron"),
        P(None, "trial", "neuron"),
        P("trial", "neuron"),
        P("trial", "neuron"),
        P("trial", "neuron"),
        P("neuron"),
        P("neuron"),
        P("neuron"),
        P("neuron"),
        P("neuron", None),
        P("neuron", None),
    )
    out_specs = (P(("neuron", "trial"), None), P(("neuron", "trial"), None))
    return jax.shard_map(shards, mesh=mesh, in_specs=in_specs, out_specs=out_specs, check_vma=False)
```

```python
import math

import jax
import jax.numpy as jnp
from jax import lax
from jax.experimental import pallas as pl
from jax.experimental.pallas import tpu as pltpu
from jax.sharding import PartitionSpec as P

sharpness = 3.0
learn_rate = 0.5

f32 = jnp.float32
bf16 = jnp.bfloat16
highest = lax.Precision.HIGHEST
block = 128
loops = 2

NN = (((1,), (0,)), ((), ()))
NT = (((1,), (1,)), ((), ()))
TN = (((0,), (0,)), ((), ()))

vmem = pl.BlockSpec(memory_space=pltpu.VMEM)


def dot(a, b, dims, precision=None):
    return lax.dot_general(a, b, dims, precision=precision, preferred_element_type=f32)


def swap(values, axes):
    return lax.all_to_all(values, axes, split_axis=0, concat_axis=0, tiled=True)


def spread(values, axes):
    copies = math.prod(lax.axis_size(a) for a in ((axes,) if isinstance(axes, str) else axes))
    return swap(jnp.broadcast_to(values[None], (copies,) + values.shape), axes)


def fire(membrane, adaptation, gain, threshold):
    level = membrane - threshold - gain * adaptation
    return 0.5 * jnp.tanh((0.5 * sharpness) * level) + 0.5


def post(total, weight, out_ref):
    total = (total * weight).astype(bf16)
    for i in range(out_ref.shape[0]):
        out_ref[i] = total


def halves(value):
    high = value.astype(bf16)
    return high, (value - high.astype(f32)).astype(bf16)


def dot3(a, b, dims):
    return dot(a[0], b[0], dims) + (dot(a[0], b[1], dims) + dot(a[1], b[0], dims))


def fetch(src_ref, dst_ref, sems, pieces):
    rows = src_ref.shape[0] // pieces
    copies = [
        pltpu.make_async_copy(
            src_ref.at[pl.ds(c * rows, rows)], dst_ref.at[pl.ds(c * rows, rows)], sems.at[c]
        )
        for c in range(pieces)
    ]
    for copy in copies:
        copy.start()
    return copies


def start_kernel(
    weight, me_ref, gain_hbm, thr_hbm, mem_hbm, ada_hbm, right_hbm, drive_hbm, learn_hbm,
    spk_ref, out_ref, right_ref, drive_ref, learn_ref, gain_ref, thr_ref, mem_ref, ada_ref, sems, sems_more,
):
    pairs = (
        (gain_hbm, gain_ref), (thr_hbm, thr_ref), (mem_hbm, mem_ref), (ada_hbm, ada_ref),
        (drive_hbm, drive_ref), (learn_hbm, learn_ref),
    )
    more = [pltpu.make_async_copy(s, d, sems_more.at[i]) for i, (s, d) in enumerate(pairs)]
    for copy in more[:4]:
        copy.start()
    copies = fetch(right_hbm, right_ref, sems, 8)
    for copy in more[4:]:
        copy.start()
    for copy in more[:4]:
        copy.wait()
    count = len(copies)
    width = right_ref.shape[0] // count

    def several(i, total):
        for c in range(2):
            c = 2 * i + c
            at = pl.ds(pl.multiple_of(c * width, width), width)
            spikes = fire(mem_ref[:, at], ada_ref[:, at], gain_ref[:, at], thr_ref[:, at])
            spk_ref[:, at] = spikes
            pltpu.make_async_copy(right_hbm.at[at], right_ref.at[at], sems.at[c]).wait()
            total = total + dot(spikes.astype(bf16), right_ref[at, :], NN)
        return total

    total = jnp.zeros((mem_ref.shape[0], right_ref.shape[1]), f32)
    post(lax.fori_loop(0, count // 2, several, total), weight, out_ref)
    for copy in more[4:]:
        copy.wait()


def step_kernel(weight_n, weight_r, moment, steps, *refs):
    first, last = moment == 0, moment + 1 == steps
    (me_ref, in_ref, dec_ref, ad_ref, gain_ref, thr_ref, drive_ref, learn_ref, mem_ref, ada_ref, fil_ref,
     spk_ref, left_ref, right_ref) = refs[:14]
    outs = refs[14:] if first else refs[16:]
    sig_ref, pre_ref = outs[:2]
    if not last:
        mem_out, ada_out, fil_out, spk_out, out_ref = outs[2:7]
    pieces, _, width = sig_ref.shape
    trials = mem_ref.shape[0]
    rows = pl.ds(moment * trials, trials)
    if first:
        left_hbm, left_ref = left_ref, outs[7]
        sems = outs[8]
        fetch(left_hbm, left_ref, sems, pieces)
    projected = jnp.sum(in_ref[...].astype(f32), 0).astype(bf16)

    def piece(c, total):
        at = pl.ds(pl.multiple_of(c * width, width), width)
        decay, threshold = dec_ref[:, at], thr_ref[:, at]
        if first:
            pltpu.make_async_copy(left_hbm.at[at], left_ref.at[at], sems.at[c]).wait()
        current = dot(projected, left_ref[at, :], NT) * weight_r
        spikes = spk_ref[:, at]
        drive = drive_ref[moment, :, at].astype(f32)
        membrane = decay * mem_ref[:, at] + drive + current - threshold * spikes
        adaptation = ad_ref[:, at] * ada_ref[:, at] + spikes
        spikes = fire(membrane, adaptation, gain_ref[:, at], threshold)
        slope = sharpness * spikes * (1.0 - spikes)
        filtered = decay * fil_ref[:, at] + spikes
        slot = me_ref[0] ^ c
        sig_ref[c, rows] = (learn_ref[moment, :, at].astype(f32) * slope).astype(bf16)
        pre_ref[slot, rows] = filtered.astype(bf16)
        if last:
            return total
        mem_out[:, at] = membrane
        ada_out[:, at] = adaptation
        fil_out[:, at] = filtered
        spk_out[:, at] = spikes
        return total + dot(spikes.astype(bf16), right_ref[at, :], NN)

    total = jnp.zeros((trials, right_ref.shape[1]), f32)

    def several(i, total):
        for c in range(pieces // loops):
            total = piece(i * (pieces // loops) + c, total)
        return total

    total = lax.fori_loop(0, loops, several, total)
    if not last:
        post(total, weight_n, out_ref)


def ranks_kernel(weight, me_ref, left_ref, right_ref, sig_ref, pre_ref, part_ref, sig_out, *refs):
    pre_outs, sems = refs[:-1], refs[-1]
    slots, _, width = sig_ref.shape
    copies = [
        pltpu.make_async_copy(pre_ref.at[s], o, sems.at[s]) for s, o in enumerate(pre_outs)
    ]
    copies.append(pltpu.make_async_copy(sig_ref, sig_out, sems.at[slots]))
    for copy in copies:
        copy.start()
    g = k = None
    for s in range(slots):
        at = pl.ds(pl.multiple_of((me_ref[0] ^ s) * width, width), width)
        a = dot(pre_ref[s], right_ref[at, :], NN)
        b = dot(sig_ref[s], left_ref[s * width : (s + 1) * width, :], NN)
        g, k = (a, b) if g is None else (g + a, k + b)
    chunk = part_ref.shape[1]
    half = g.shape[0] // chunk
    for i in range(half):
        part_ref[i] = (g[i * chunk : (i + 1) * chunk] * weight).astype(bf16)
        part_ref[half + i] = (k[i * chunk : (i + 1) * chunk] * weight).astype(bf16)
    for copy in copies:
        copy.wait()


def again_kernel(in_ref, out_ref):
    total = jnp.sum(in_ref[...].astype(f32), 0).astype(out_ref.dtype)
    for i in range(out_ref.shape[0]):
        out_ref[i] = total


def gradient(weight, slots, me_ref, factor_hbm, ranks, pieces, rows, near, held, sem, sems, use):
    width = rows.shape[0]
    deep = pieces[0].shape[0]
    copies = []
    for s in range(slots):
        at = pl.ds(s * deep, deep)
        for i, (src, dst) in enumerate(((ranks[s], near), (pieces[s], held))):
            copies.append(pltpu.make_async_copy(src, dst.at[at], sems.at[i, s]))
    copies.append(
        pltpu.make_async_copy(
            factor_hbm.at[pl.ds(pl.multiple_of(me_ref[0] * width, width), width)], rows, sem
        )
    )
    for copy in copies:
        copy.start()
    for copy in copies:
        copy.wait()
    size = 4 * block

    def several(i, carry):
        at = pl.ds(pl.multiple_of(i * size, size), size)
        use(at, rows[at].astype(f32) - weight * dot(held[:, at], near[...], TN))
        return carry

    lax.fori_loop(0, width // size, several, 0)


def packing(n):
    return [(o, n - block - o) for o in range(0, n // 2, block)]


def right_kernel(weight, slots, me_ref, factor_hbm, *refs):
    high_hbm, low_hbm, gram_ref = refs[2 * slots : 2 * slots + 3]
    rows, near, held, high, low, sem, sems, out_sem = refs[2 * slots + 3 :]

    def use(at, step):
        high[at], low[at] = halves(step)

    gradient(
        weight, slots, me_ref, factor_hbm, refs[:slots], refs[slots : 2 * slots], rows, near, held, sem, sems, use
    )
    back = [
        pltpu.make_async_copy(v, o, out_sem.at[i])
        for i, (v, o) in enumerate(((high, high_hbm), (low, low_hbm)))
    ]
    for copy in back:
        copy.start()
    n = high.shape[1]
    for group in packing(n):
        packed = jnp.concatenate(
            [
                dot3(
                    (high[:, o : o + block], low[:, o : o + block]), (high[:, o:], low[:, o:]), TN
                )
                + dot(low[:, o : o + block], low[:, o:], TN)
                for o in group
            ],
            1,
        )
        at = group[0] // 2
        for i in range(block // 2):
            gram_ref[at + i] = packed[2 * i : 2 * i + 2]
    for copy in back:
        copy.wait()


def left_kernel(weight, weight_l, slots, me_ref, high_ref, low_ref, factor_hbm, *refs):
    ranks, signal_hbm, out_ref, (rows, near, held, sem, sems) = (
        refs[:slots], refs[slots], refs[slots + 1], refs[slots + 2 :]
    )
    pieces = [signal_hbm.at[me_ref[0] ^ s] for s in range(slots)]
    upper = high_ref[...], low_ref[...]

    def use(at, step):
        out_ref[at] = (dot3(halves(step), upper, NT) * weight_l).astype(bf16)

    gradient(weight, slots, me_ref, factor_hbm, ranks, pieces, rows, near, held, sem, sems, use)


def diagonal(rows):
    groups = len(rows)
    wide = (8, block)
    lane = lax.broadcasted_iota(jnp.int32, wide, 1)
    sub = lax.broadcasted_iota(jnp.int32, wide, 0)
    rows = list(rows)
    ones = [jnp.where(lane == sub + 8 * g, 1.0, 0.0).astype(f32) for g in range(groups)]
    for g in range(groups):
        cols = [jnp.broadcast_to(rows[g][:, 8 * g + k : 8 * g + k + 1], wide) for k in range(8)]
        pivots = []
        a, e, root = rows[g], ones[g], None
        for j in range(8):
            d = jnp.broadcast_to(cols[j][j : j + 1, :], wide)
            inverse = 1.0 / d
            col = jnp.where(sub > j, cols[j], 0.0)
            us = [None] * 8
            for k in range(j + 1, 8):
                us[k] = jnp.broadcast_to(cols[k][j : j + 1, :], wide)
                cols[k] = cols[k] - (col * us[k]) * inverse
            ua = jnp.broadcast_to(a[j : j + 1, :], wide)
            ue = jnp.broadcast_to(e[j : j + 1, :], wide)
            m = col * inverse
            a = a - m * ua
            e = e - m * ue
            r = lax.rsqrt(d)
            root = r if root is None else jnp.where(sub == j, r, root)
            pivots.append((inverse, us, ua, ue))
        ones[g] = e * root
        for h in range(g + 1, groups):
            cols = [jnp.broadcast_to(rows[h][:, 8 * g + k : 8 * g + k + 1], wide) for k in range(8)]
            a, e = rows[h], ones[h]
            for j in range(8):
                inverse, us, ua, ue = pivots[j]
                m = cols[j] * inverse
                for k in range(j + 1, 8):
                    cols[k] = cols[k] - m * us[k]
                a = a - m * ua
                e = e - m * ue
            rows[h], ones[h] = a, e
    return ones


def finish_kernel(weight_r, gram_ref, rh, rl, upper_hi, upper_lo, right_ref, aug, part, steps, sems):
    n = right_ref.shape[1]
    blocks = n // block
    copies = [pltpu.make_async_copy(v, steps.at[i], sems.at[i]) for i, v in enumerate((rh, rl))]
    for copy in copies:
        copy.start()
    row = lax.broadcasted_iota(jnp.int32, (n, n), 0)
    col = lax.broadcasted_iota(jnp.int32, (n, n), 1)
    for group in packing(n):
        for i in range(block // 2):
            pair, at = gram_ref[group[0] // 2 + i], 0
            for o in group:
                aug[o + 2 * i : o + 2 * i + 2, o:n] = pair[:, at : at + n - o]
                at += n - o
    aug[:, n:] = jnp.where(row == col, 1.0, 0.0).astype(f32)

    def panel(p, carry):
        o = pl.multiple_of(p * block, block)
        ones = diagonal(
            [
                aug[pl.ds(pl.multiple_of(o + 8 * g, 8), 8), pl.ds(o, block)]
                for g in range(block // 8)
            ]
        )
        for g in range(block // 8):
            part[8 * g : 8 * g + 8, :] = ones[g]
        for k in range(blocks):

            @pl.when(p == k)
            def _(k=k):
                lo = k * block
                new = dot(part[...], aug[lo : lo + block, lo : n + lo + block], NN, highest)
                aug[lo : lo + block, lo : n + lo + block] = new
                if k + 1 < blocks:
                    aug[lo + block :, lo + block : n + lo + block] -= dot(
                        new[:, block : n - lo], new[:, block:], TN, highest
                    )

        return carry

    lax.fori_loop(0, blocks, panel, 0)
    upper_hi[...], upper_lo[...] = halves(jnp.where(row <= col, aug[:, :n], 0.0))
    inverse = halves(jnp.where(row >= col, aug[:, n:], 0.0))
    for copy in copies:
        copy.wait()
    right_ref[...] = (dot3((steps[0], steps[1]), inverse, NT) * weight_r).astype(bf16)


def call(kernel, args, outs, name, limit, scratch=(), aliases=None, far=(), far_outs=(), flops=None):
    hbm = pl.BlockSpec(memory_space=pltpu.HBM)
    smem = pl.BlockSpec(memory_space=pltpu.SMEM)
    args = [
        pltpu.with_memory_space_constraint(a, pltpu.HBM) if i in far else a
        for i, a in enumerate(args)
    ]
    outs = [
        pltpu.HBM(o.shape, o.dtype) if i in far_outs else o for i, o in enumerate(outs)
    ]
    return pl.pallas_call(
        kernel,
        out_shape=outs,
        in_specs=[
            smem if a.dtype == jnp.int32 else hbm if i in far else vmem for i, a in enumerate(args)
        ],
        out_specs=[hbm if i in far_outs else vmem for i in range(len(outs))],
        scratch_shapes=scratch,
        input_output_aliases=aliases or {},
        name=name,
        cost_estimate=flops and pl.CostEstimate(flops=flops, transcendentals=0, bytes_accessed=0),
        compiler_params=pltpu.CompilerParams(vmem_limit_bytes=limit << 20),
    )(*args)


def shards(
    drive,
    learning,
    membrane_init,
    adapt_init,
    trace_init,
    membrane_decay,
    adapt_decay,
    adapt_gain,
    threshold,
    left_factor,
    right_factor,
):
    local_neurons, rank_width = left_factor.shape
    step_count, local_trials = drive.shape[:2]
    neuron_shards = lax.axis_size("neuron")
    trial_shards = lax.axis_size("trial")
    neuron_count = local_neurons * neuron_shards
    norm_neurons = 1.0 / math.sqrt(neuron_count)
    norm_rank = 1.0 / math.sqrt(rank_width)
    stored = local_neurons // trial_shards
    struct = jax.ShapeDtypeStruct
    decay, adecay, gain, level = (
        v.reshape(1, -1) for v in (membrane_decay, adapt_decay, adapt_gain, threshold)
    )
    state = pltpu.VMEM(membrane_init.shape, f32)
    sent = struct((neuron_shards, local_trials, rank_width), bf16)
    rows = step_count * local_trials
    slots = trial_shards
    everyone = ("neuron", "trial")
    me = lax.axis_index("trial").astype(jnp.int32).reshape(1)
    copy_sem = pltpu.SemaphoreType.DMA

    spikes, out, right_near, drive_near, learn_near = call(
        lambda *r: start_kernel(norm_neurons, *r),
        (me, gain, level, membrane_init, adapt_init, right_factor, drive, learning),
        [
            state,
            sent,
            pltpu.VMEM(right_factor.shape, bf16),
            pltpu.VMEM(drive.shape, bf16),
            pltpu.VMEM(learning.shape, bf16),
        ],
        "start",
        8,
        (
            pltpu.VMEM(gain.shape, f32),
            pltpu.VMEM(level.shape, f32),
            pltpu.VMEM(membrane_init.shape, f32),
            pltpu.VMEM(adapt_init.shape, f32),
            copy_sem((8,)),
            copy_sem((6,)),
        ),
        far=tuple(range(1, 8)),
    )
    states = [membrane_init, adapt_init, trace_init, spikes]
    kept = pltpu.VMEM((slots, rows, stored), bf16)
    left_near = left_factor
    every = ()

    def exchange(values, k):
        return lax.ppermute(values, "trial", [(i, i ^ k) for i in range(slots)]) if k else values

    for moment in range(step_count):
        first, last = moment == 0, moment + 1 == step_count
        got = swap(out, "neuron")
        result = call(
            lambda *r, moment=moment: step_kernel(norm_neurons, norm_rank, moment, step_count, *r),
            (me, got, decay, adecay, gain, level, drive_near, learn_near, *states, left_near, right_near, *every),
            [kept, kept]
            + ([] if last else [state, state, state, state, sent])
            + ([pltpu.VMEM(left_factor.shape, bf16)] if first else []),
            "step",
            8,
            (copy_sem((slots,)),) if first else (),
            {} if first else {14: 0, 15: 1} | ({} if last else {8 + i: 2 + i for i in range(4)}),
            (12,) if first else (),
        )
        every = result[:2]
        if not last:
            states, out = result[2:6], result[6]
        if first:
            left_near = result[7]

    chunk = 2 * rows // neuron_shards
    slot = struct((rows, stored), bf16)
    part, signal_all, *presyn_mine = call(
        lambda *r: ranks_kernel(norm_neurons, *r),
        (me, left_near, right_near, *every),
        [struct((neuron_shards, chunk, rank_width), bf16), struct((slots, rows, stored), bf16)]
        + [slot] * slots,
        "ranks",
        16,
        (copy_sem((slots + 1,)),),
        far_outs=tuple(range(1, 2 + slots)),
    )
    down = [(i, (i - 2) % slots) for i in range(slots)]
    over = [(i, ((i - 2) % slots) ^ 1) for i in range(slots)]
    opposite = {4: exchange(presyn_mine[4], 4), 5: lax.ppermute(presyn_mine[5], "trial", down)}
    presyn_mine = [opposite[k] if k in opposite else exchange(v, k) for k, v in enumerate(presyn_mine)]

    def again(blocks, copies):
        return call(
            again_kernel,
            (blocks,),
            [struct((copies,) + blocks.shape[1:], blocks.dtype)],
            "again",
            8,
        )[0]

    def everywhere(values):
        same = [exchange(values, 2 * j) for j in range(slots // 2)]
        return [v for s in same for v in (s, exchange(s, 1))]

    mine = again(swap(part, "neuron"), neuron_shards)
    near = [4, 5, 2, 3, 6]
    mine, *moved = lax.optimization_barrier((mine, *[presyn_mine[k] for k in near]))
    for k, v in zip(near, moved, strict=True):
        presyn_mine[k] = v
    presyn_mine[5] = lax.ppermute(presyn_mine[5], "trial", over)
    ranks = swap(mine, "neuron")
    ranks = ranks.reshape(2, rows, rank_width)
    rank_g = ranks[0]
    pair = struct((stored, rank_width), bf16)
    blocks = struct((rank_width // 4, 2, rank_width + block), f32)
    weight = learn_rate * norm_rank

    far = 2 * slots + 1
    scratch = (
        pltpu.VMEM((stored, rank_width), bf16),
        pltpu.VMEM((slots * rows, rank_width), bf16),
        pltpu.VMEM((slots * rows, stored), bf16),
    )
    sems = (copy_sem, copy_sem((2, slots)))
    right_hi, right_lo, gram_part = call(
        lambda *r: right_kernel(weight, slots, *r),
        (me, right_factor, *everywhere(ranks[1]), *presyn_mine),
        [pair, pair, blocks],
        "right",
        32,
        (*scratch, *scratch[:1], *scratch[:1], *sems, copy_sem((2,))),
        far=tuple(range(1, 1 + far)),
        far_outs=(0, 1),
    )
    gram_one = swap(again(swap(gram_part, everyone), neuron_shards * slots), everyone)
    gram_one, signal_all, rank_g = lax.optimization_barrier((gram_one, signal_all, rank_g))
    signal_mine = swap(signal_all, "trial")
    rank_g = everywhere(rank_g)
    square = struct((rank_width, rank_width), bf16)
    upper_hi, upper_lo, right_new = call(
        lambda *r: finish_kernel(math.sqrt(neuron_count), *r),
        (gram_one, right_hi, right_lo),
        [square, square, pair],
        "finish",
        24,
        (
            pltpu.VMEM((rank_width, 2 * rank_width), f32),
            pltpu.VMEM((block, block), f32),
            pltpu.VMEM((2, stored, rank_width), bf16),
            copy_sem((2,)),
        ),
        far=(1, 2),
        flops=20 * 10**9,
    )
    (left_new,) = call(
        lambda *r: left_kernel(weight, norm_neurons, slots, *r),
        (me, upper_hi, upper_lo, left_factor, *rank_g, signal_mine),
        [pair],
        "left",
        32,
        (*scratch, *sems),
        far=tuple(range(3, 5 + slots)),
    )
    return (left_new, right_new)


def solution(mesh):
    in_specs = (
        P(None, "trial", "neuron"),
        P(None, "trial", "neuron"),
        P("trial", "neuron"),
        P("trial", "neuron"),
        P("trial", "neuron"),
        P("neuron"),
        P("neuron"),
        P("neuron"),
        P("neuron"),
        P("neuron", None),
        P("neuron", None),
    )
    out_specs = (P(("neuron", "trial"), None), P(("neuron", "trial"), None))
    return jax.shard_map(shards, mesh=mesh, in_specs=in_specs, out_specs=out_specs, check_vma=False)
```
